32 devices in a mesh: ctx: 16 (over z, y, core), fsdp: 2 (over x).
Axes of the slice: x: 2, y: 2, z: 4, core: 2. Of those that a mesh axis runs over, the one named last changes fastest.
Arguments:
- queries: bfloat16 [2, 2048, 2048], P('fsdp', 'ctx'), may hold values from -8 to 8
- keys_values: bfloat16 [2, 2048, 2, 2048], P('fsdp', 'ctx'), may hold values from -8 to 8
- upstream: bfloat16 [2, 2048, 2048], P('fsdp', 'ctx'), may hold values from -6 to 6
- out_weight: bfloat16 [2048, 2048], P('fsdp'), may hold values from -0.125 to 0.125
Outputs:
- grad_queries: bfloat16 [2, 2048, 2048], P('fsdp', 'ctx')
- grad_keys_values: bfloat16 [2, 2048, 2, 2048], P('fsdp', 'ctx')
- grad_weight: float32 [2048, 2048], P(('ctx', 'fsdp'))
The draws below stay inside these ranges and needn't reach their ends.
All inputs are finite; a program needn't handle non-finite values.
Results may differ from the reference program's by a relative error of at most 0.014.
Values may be sent and summed in bfloat16 or wider, within the bound.
A program may use at most 128 MiB of HBM per device.

```python
import jax
import jax.numpy as jnp
from jax import lax

D = 2048
HEADS = 16
HEAD_DIM = 128
ATTN = 2048
TOK_DEV = 128
SPAN = 4
WINDOW = 512
SEQ_DEV = 1
SEQ = 2048
SEQS = 2
N_CTX = 16
N_FSDP = 2


def draw_queries(key, part):
    result = jnp.clip(jax.random.normal(jax.random.fold_in(key, 11), (SEQS, SEQ, ATTN), jnp.float32), -4.0, 4.0)
    return result.astype(jnp.bfloat16)


def draw_keys_values(key, part):
    key_part = jnp.clip(jax.random.normal(jax.random.fold_in(key, 21), (SEQS, SEQ, ATTN), jnp.float32), -4.0, 4.0)
    value_part = jnp.clip(jax.random.normal(jax.random.fold_in(key, 23), (SEQS, SEQ, ATTN), jnp.float32), -4.0, 4.0)
    return jnp.stack([key_part, value_part], axis=2).astype(jnp.bfloat16)


def spiked(values, own_key, source, target, parts, factor):
    def block_of(axis_at):
        return (jnp.arange(values.shape[axis_at]) // (values.shape[axis_at] // parts)).reshape((-1,) + (1,) * (values.ndim - 1 - axis_at))

    near = jax.random.permutation(own_key, parts)[block_of(target)]
    other_side = (block_of(target) + parts // 2) % parts
    return jnp.where((block_of(source) == near) | (block_of(source) == other_side), factor * values, values)


def levels(stream_key, dims, cuts, smallest, top_value):
    level, own = 1.0, jax.random.fold_in(stream_key, 6)
    for axis_at, parts in cuts:
        steps = jnp.exp(jax.random.uniform(jax.random.fold_in(own, axis_at), (parts,), jnp.float32, smallest / len(cuts), top_value / len(cuts)))
        level = level * jnp.repeat(steps, dims[axis_at] // parts).reshape([-1 if axis == axis_at else 1 for axis in range(len(dims))])
    return level


def scatter_about(rng, shape, width, reach, split=(), kind=jnp.bfloat16):
    drawn = jax.random.normal(rng, shape, jnp.float32) * width
    if len(split) > 0:
        drawn = levels(rng, shape, split, -0.22, 0.18) * drawn
    return jnp.clip(drawn, min=-reach, max=reach).astype(kind)


def gaussian_with(own_key, dims, width, bound, cuts, heavy, kind=jnp.bfloat16):
    values = width * jax.random.normal(own_key, dims, jnp.float32)
    if cuts:
        values = values * levels(own_key, dims, cuts, -0.22, 0.18)
    return jnp.clip(spiked(values, jax.random.fold_in(own_key, 3), *heavy), -bound, bound).astype(kind)


def setup_inputs(seed: int = 0) -> dict:
    key_of = jax.random.split(jax.random.key(seed), 5)
    queries = draw_queries(jax.random.fold_in(key_of[4], 71), 0)
    keys_values = draw_keys_values(jax.random.fold_in(key_of[4], 71), 0)
    upstream = gaussian_with(key_of[2], (SEQS, SEQ, D), 1.0, 6.0, ((0, 2), (1, 16)), (1, 2, 16, 2.0))
    out_weight = scatter_about(key_of[3], (D, ATTN), ATTN ** -0.5, 0.125, ((0, 2),))
    return {"queries": queries, "keys_values": keys_values, "upstream": upstream, "out_weight": out_weight}


NEGATIVE = -1e30


def one_sequence(inputs):
    query_seq, pair_seq, grad_seq = inputs
    padding = SPAN * TOK_DEV
    key_count = (SPAN + 1) * TOK_DEV
    inv_root = HEAD_DIM ** -0.5
    padded_pairs = jnp.concatenate([jnp.zeros((padding, 2, ATTN), jnp.bfloat16), pair_seq], axis=0)

    def block_step(carried, block_index):
        first_row = (block_index * TOK_DEV).astype(jnp.int32)
        query_block = lax.dynamic_slice_in_dim(query_seq, first_row, TOK_DEV, 0).astype(jnp.float32).reshape(TOK_DEV, HEADS, HEAD_DIM)
        grad_block = lax.dynamic_slice_in_dim(grad_seq, first_row, TOK_DEV, 0).reshape(TOK_DEV, HEADS, HEAD_DIM)
        pair_window = lax.dynamic_slice_in_dim(padded_pairs, first_row, key_count, 0)
        key_heads = pair_window[:, 0].astype(jnp.float32).reshape(key_count, HEADS, HEAD_DIM)
        value_heads = pair_window[:, 1].astype(jnp.float32).reshape(key_count, HEADS, HEAD_DIM)
        query_pos = first_row + jnp.arange(TOK_DEV, dtype=jnp.int32)
        key_pos = first_row - padding + jnp.arange(key_count, dtype=jnp.int32)
        distance = query_pos[:, None] - key_pos[None, :]
        visible = (distance >= 0) & (distance < WINDOW) & (key_pos[None, :] >= 0)
        scores = jnp.einsum('qhe,khe->hqk', query_block, key_heads) * inv_root
        scores = jnp.where(visible[None], scores, NEGATIVE)
        row_max = jnp.max(scores, axis=-1, keepdims=True)
        lifted = jnp.exp(scores - row_max)
        probability = lifted / jnp.sum(lifted, axis=-1, keepdims=True)
        probs_low = probability.astype(jnp.bfloat16)
        attended = jnp.einsum('hqk,khe->qhe', probs_low.astype(jnp.float32), value_heads).astype(jnp.bfloat16)
        grad_f = grad_block.astype(jnp.float32)
        products = jnp.einsum('qhe,khe->hqk', grad_f, value_heads)
        center = jnp.sum(grad_f * attended.astype(jnp.float32), axis=-1)
        center = jnp.swapaxes(center, 0, 1)[:, :, None]
        grad_scores = (probability * (products - center)).astype(jnp.bfloat16).astype(jnp.float32)
        grad_queries = (jnp.einsum('hqk,khe->qhe', grad_scores, key_heads) * inv_root).astype(jnp.bfloat16)
        grad_keys = jnp.einsum('hqk,qhe->khe', grad_scores, query_block) * inv_root
        grad_values = jnp.einsum('hqk,qhe->khe', probs_low.astype(jnp.float32), grad_f)
        grad_window = jnp.stack([grad_keys.reshape(key_count, ATTN), grad_values.reshape(key_count, ATTN)], axis=1)
        previous = lax.dynamic_slice_in_dim(carried, first_row, key_count, 0)
        carried = lax.dynamic_update_slice_in_dim(carried, previous + grad_window, first_row, 0)
        return carried, (attended.reshape(TOK_DEV, ATTN), grad_queries.reshape(TOK_DEV, ATTN))

    start_carry = jnp.zeros((SEQ + padding, 2, ATTN), jnp.float32)
    carried, outputs = lax.scan(block_step, start_carry, jnp.arange(N_CTX, dtype=jnp.int32))
    attended_all = outputs[0].reshape(SEQ, ATTN)
    grad_query_all = outputs[1].reshape(SEQ, ATTN)
    return attended_all, grad_query_all, carried[padding:].astype(jnp.bfloat16)


def reference(queries, keys_values, upstream, out_weight):
    grad_attended = jnp.dot(upstream.reshape(SEQS * SEQ, D), out_weight, preferred_element_type=jnp.float32)
    grad_attended = grad_attended.astype(jnp.bfloat16).reshape(SEQS, SEQ, ATTN)
    attended, grad_queries, grad_keys_values = lax.map(one_sequence, (queries, keys_values, grad_attended))
    attended_dev = attended.reshape(N_FSDP, SEQ_DEV, N_CTX, TOK_DEV, ATTN).transpose(0, 2, 1, 3, 4)
    attended_dev = attended_dev.reshape(N_FSDP * N_CTX, SEQ_DEV * TOK_DEV, ATTN)
    upstream_dev = upstream.reshape(N_FSDP, SEQ_DEV, N_CTX, TOK_DEV, D).transpose(0, 2, 1, 3, 4)
    upstream_dev = upstream_dev.reshape(N_FSDP * N_CTX, SEQ_DEV * TOK_DEV, D)

    def add_partial(running, pieces):
        weight_term = lax.dot_general(pieces[0], pieces[1], (((0,), (0,)), ((), ())), preferred_element_type=jnp.float32)
        weight_term = lax.optimization_barrier(weight_term.astype(jnp.bfloat16)).astype(jnp.float32)
        return running + weight_term, None

    grad_weight, unused_out = lax.scan(add_partial, jnp.zeros((D, ATTN), jnp.float32), (upstream_dev, attended_dev))
    return grad_queries, grad_keys_values, grad_weight
```

```python
import functools

import jax
import jax.numpy as jnp
from jax import lax
from jax.experimental import pallas as pl
from jax.experimental.pallas import tpu as pltpu
from jax.sharding import PartitionSpec as P

HEAD_DIM = 128
SPAN = 4
NEGATIVE = -1e30
F32 = jnp.float32
BF16 = jnp.bfloat16
NT = (((1,), (1,)), ((), ()))
TN = (((0,), (0,)), ((), ()))


def remote(src, dst, send, recv, device):
    return pltpu.make_async_remote_copy(
        src_ref=src, dst_ref=dst, send_sem=send, recv_sem=recv, device_id=device, device_id_type=pl.DeviceIdType.MESH
    )


def layer_kernel(
    planes, fsdp,
    q_in, kv_in, up_in, weight,
    dq_out, kv_out, out_w,
    q, kv, up, up_t, w, ga, att, low, bias, dq, dkv, dprev, dprev_in, dsum,
    gw_out, gw_in, zw_out, zw_in, fin_out, fin_in,
    own_sem, kv_s, kv_r, q_s, q_r, u_s, u_r, w_s, w_r, kz_s, kz_r,
    dq_s, dq_r, dz_s, dz_r, dk_s, dk_r, gx_s, gx_r, gz_s, gz_r, f_s, f_r,
):
    toks = q_in.shape[0]
    depth = weight.shape[0]
    width = weight.shape[1]
    quarter = width // SPAN
    heads = quarter // HEAD_DIM
    plane_toks = SPAN * toks
    keys = plane_toks + toks
    own_rows = out_w.shape[0]
    plane_rows = SPAN * own_rows
    inv_root = HEAD_DIM ** (-0.5)

    me = lax.axis_index("ctx")
    f = lax.axis_index("fsdp")
    p = lax.div(me, SPAN)
    r = lax.rem(me, SPAN)
    mate = r + 1 - 2 * lax.rem(r, 2)
    peer = [r, mate, lax.rem(r + 2, SPAN), lax.rem(mate + 2, SPAN)]
    not_first = p > 0
    not_last = p < planes - 1

    def dev(p_, r_, f_):
        return {"ctx": p_ * SPAN + r_, "fsdp": f_}

    def near(d):
        return dev(p, peer[d], f)

    def side(df):
        return lax.rem(f + df, fsdp)

    def level(dp):
        return lax.rem(p + dp, planes)

    def rows(i):
        return pl.ds(pl.multiple_of(i * toks, toks), toks)

    def own_plane(i):
        return pl.ds(pl.multiple_of(plane_toks + i * toks, toks), toks)

    def head(c):
        return pl.ds(c * HEAD_DIM, HEAD_DIM)

    def wide_head(i, c):
        return pl.ds(pl.multiple_of(i * quarter + c * HEAD_DIM, HEAD_DIM), HEAD_DIM)

    def quart(i):
        return pl.ds(pl.multiple_of(i * quarter, quarter), quarter)

    def w_rows(i):
        return pl.ds(pl.multiple_of(i * depth, depth), depth)

    own_copies = [
        pltpu.make_async_copy(kv_in.at[:, :, quart(r)], kv.at[:, own_plane(r), :], own_sem.at[0]),
        pltpu.make_async_copy(q_in.at[:, quart(r)], q.at[rows(r), :], own_sem.at[1]),
        pltpu.make_async_copy(up_in, up.at[rows(r), :], own_sem.at[2]),
        pltpu.make_async_copy(weight.at[:, quart(r)], w.at[w_rows(f), :], own_sem.at[3]),
    ]
    for copy in own_copies:
        copy.start()

    sem = pltpu.get_barrier_semaphore()
    targets = [near(d) for d in range(1, SPAN)]
    targets += [dev(p, r, side(df)) for df in range(1, fsdp)]
    targets += [dev(level(dp), r, f) for dp in range(1, planes)]
    for target in targets:
        pl.semaphore_signal(sem, inc=1, device_id=target, device_id_type=pl.DeviceIdType.MESH)
    pl.semaphore_wait(sem, len(targets))

    def kv_copy(d, c):
        return remote(kv_in.at[:, :, wide_head(peer[d], c)], kv.at[:, own_plane(r), head(c)], kv_s.at[d, c], kv_r.at[d, c], near(d))

    def kv_came(d, c):
        here = kv.at[:, own_plane(peer[d]), head(c)]
        remote(here, here, kv_s.at[d, c], kv_r.at[d, c], near(d)).wait_recv()

    def q_copy(d, c):
        return remote(q_in.at[:, wide_head(peer[d], c)], q.at[rows(r), head(c)], q_s.at[d, c], q_r.at[d, c], near(d))

    def q_came(d, c):
        here = q.at[rows(peer[d]), head(c)]
        remote(here, here, q_s.at[d, c], q_r.at[d, c], near(d)).wait_recv()

    def up_copy(d):
        if d == 3:
            here = up.at[rows(peer[2]), :]
            return remote(here, here, u_s.at[3], u_r.at[3], near(1))
        return remote(up_in, up.at[rows(r), :], u_s.at[d], u_r.at[d], near(d))

    def up_came(d):
        here = up.at[rows(peer[d]), :]
        remote(here, here, u_s.at[d], u_r.at[d], near(d)).wait_recv()

    def w_copy(df, c):
        return remote(
            weight.at[:, wide_head(r, c)], w.at[w_rows(f), head(c)], w_s.at[df, c], w_r.at[fsdp - df, c], dev(p, r, side(df))
        )

    def w_came(df, c):
        here = w.at[w_rows(side(df)), head(c)]
        remote(here, here, w_s.at[df, c], w_r.at[df, c], dev(p, r, side(df))).wait_recv()

    def kz_copy(d, c):
        src = kv_in.at[:, :, wide_head(r, c)] if d == 0 else kv.at[:, own_plane(peer[d]), head(c)]
        return remote(src, kv.at[:, rows(peer[d]), head(c)], kz_s.at[d, c], kz_r.at[d, c], dev(p + 1, r, f))

    def dq_copy(d, c):
        return remote(dq.at[rows(peer[d]), head(c)], dq_out.at[:, wide_head(r, c)], dq_s.at[d, c], dq_r.at[d, c], near(d))

    def dq_came(d, c):
        here = dq_out.at[:, wide_head(peer[d], c)]
        remote(here, here, dq_s.at[d, c], dq_r.at[d, c], near(d)).wait_recv()

    def own_dq(c):
        return pltpu.make_async_copy(dq.at[rows(r), head(c)], dq_out.at[:, wide_head(r, c)], dq_s.at[0, c])

    def dz_copy(c):
        return remote(dprev.at[:, :, head(c)], dprev_in.at[:, :, head(c)], dz_s.at[c], dz_r.at[c], dev(p - 1, r, f))

    def dk_copy(d, c):
        return remote(dsum.at[:, rows(peer[d]), head(c)], kv_out.at[:, :, wide_head(r, c)], dk_s.at[d, c], dk_r.at[d, c], near(d))

    def dk_came(d, c):
        here = kv_out.at[:, :, wide_head(peer[d], c)]
        remote(here, here, dk_s.at[d, c], dk_r.at[d, c], near(d)).wait_recv()

    def own_dk(c):
        return pltpu.make_async_copy(dsum.at[:, rows(r), head(c)], kv_out.at[:, :, wide_head(r, c)], dk_s.at[0, c])

    def gx_copy(df, c):
        return remote(
            gw_out.at[side(df), :, head(c)], gw_in.at[fsdp - df, :, head(c)], gx_s.at[df, c], gx_r.at[fsdp - df, c],
            dev(p, r, side(df)),
        )

    def gx_came(df, c):
        here = gw_in.at[df, :, head(c)]
        remote(here, here, gx_s.at[df, c], gx_r.at[df, c], dev(p, r, side(df))).wait_recv()

    def gz_copy(dp, c):
        return remote(
            zw_out.at[level(dp), :, head(c)], zw_in.at[planes - dp, :, head(c)], gz_s.at[dp, c], gz_r.at[planes - dp, c],
            dev(level(dp), r, f),
        )

    def gz_came(dp, c):
        here = zw_in.at[dp, :, head(c)]
        remote(here, here, gz_s.at[dp, c], gz_r.at[dp, c], dev(level(dp), r, f)).wait_recv()

    def f_copy(d, c):
        return remote(fin_out.at[peer[d], :, head(c)], fin_in.at[r, :, head(c)], f_s.at[d, c], f_r.at[d, c], near(d))

    def f_came(d, c):
        here = fin_in.at[peer[d], :, head(c)]
        remote(here, here, f_s.at[d, c], f_r.at[d, c], near(d)).wait_recv()

    around = range(1, SPAN)

    def spread(c):
        for d in around:
            kv_copy(d, c).start()
        for d in around:
            q_copy(d, c).start()

    for c in range(heads):
        @pl.when(not_last)
        def _(c=c):
            kz_copy(0, c).start()

        for df in range(1, fsdp):
            w_copy(df, c).start()
        spread(c)
        if c == 1:
            up_copy(2).start()
            up_copy(1).start()

    row = lax.broadcasted_iota(jnp.int32, (toks, keys), 0)
    col = lax.broadcasted_iota(jnp.int32, (toks, keys), 1)
    for b in range(SPAN):
        first = jnp.where(not_first, 0, plane_toks - b * toks)
        bias[b] = jnp.where((col > row) & (col <= row + plane_toks) & (col >= first), 0.0, NEGATIVE)
    dkv[...] = jnp.zeros(dkv.shape, F32)

    @pl.when(p == 0)
    def _():
        kv[:, :plane_toks] = jnp.zeros((2, plane_toks, quarter), BF16)

    def forward(c):
        for d in around:
            kv_came(d, c)

            @pl.when(not_last)
            def _(d=d):
                kz_copy(d, c).start()

    def window(b):
        return pl.ds(b * toks, keys)

    def attend(c):
        for d in around:
            q_came(d, c)

        @pl.when(not_first)
        def _():
            for d in range(SPAN):
                here = kv.at[:, rows(peer[d]), head(c)]
                remote(here, here, kz_s.at[d, c], kz_r.at[d, c], near(1)).wait_recv()

        for b in range(SPAN):
            block = pl.ds(b * toks, toks)
            scores = lax.dot_general(q[block, head(c)], kv[0, window(b), head(c)], NT, preferred_element_type=F32) * inv_root + bias[b]
            lifted = jnp.exp(scores - jnp.max(scores, axis=-1, keepdims=True))
            prob = (lifted * (1.0 / jnp.sum(lifted, axis=-1, keepdims=True))).astype(BF16)
            low[c * SPAN + b] = prob
            att[block, head(c)] = jnp.dot(prob, kv[1, window(b), head(c)], preferred_element_type=F32).astype(BF16)

    def backward(c):
        for b in range(SPAN):
            block = pl.ds(b * toks, toks)
            g = ga[block, head(c)]
            prob = low[c * SPAN + b]
            k = kv[0, window(b), head(c)]
            products = lax.dot_general(g, kv[1, window(b), head(c)], NT, preferred_element_type=F32)
            center = jnp.sum(g.astype(F32) * att[block, head(c)].astype(F32), axis=-1, keepdims=True)
            ds = (prob.astype(F32) * (products - center)).astype(BF16)
            dq[block, head(c)] = (jnp.dot(ds, k, preferred_element_type=F32) * inv_root).astype(BF16)
            dkv[0, window(b), head(c)] += lax.dot_general(ds, q[block, head(c)], TN, preferred_element_type=F32) * inv_root
            dkv[1, window(b), head(c)] += lax.dot_general(prob, g, TN, preferred_element_type=F32)
        for d in (2, 3, 1):
            dq_copy(d, c).start()
        own_dq(c).start()
        dprev[:, :, head(c)] = dkv[:, :plane_toks, head(c)].astype(BF16)

        @pl.when(not_first)
        def _():
            dz_copy(c).start()

    def collect(c):
        @pl.when(not_last)
        def _():
            dz_copy(c).wait_recv()
            dsum[:, :, head(c)] = (dkv[:, plane_toks:, head(c)] + dprev_in[:, :, head(c)].astype(F32)).astype(BF16)

        @pl.when(p == planes - 1)
        def _():
            dsum[:, :, head(c)] = dkv[:, plane_toks:, head(c)].astype(BF16)

        for d in (2, 3, 1):
            dk_copy(d, c).start()
        own_dk(c).start()

    pair = 2 * HEAD_DIM

    def project(g):
        for c in (2 * g, 2 * g + 1):
            for df in range(1, fsdp):
                w_came(df, c)
        for b in range(SPAN):
            block = pl.ds(b * toks, toks)
            ga[block, g * pair : (g + 1) * pair] = jnp.dot(
                up[block, :], w[:, g * pair : (g + 1) * pair], preferred_element_type=F32
            ).astype(BF16)

    tile = plane_toks
    unit = fsdp * own_rows

    def weigh(g):
        cols = slice(g * pair, (g + 1) * pair)

        def step(t, _):
            value = jnp.dot(up_t[pl.ds(pl.multiple_of(t * tile, tile), tile), :], att[:, cols], preferred_element_type=F32)
            value = value.reshape(tile // unit, fsdp, own_rows, pair)
            part = tile // fsdp
            for n in range(fsdp):
                gw_out[n, pl.ds(pl.multiple_of(t * part, part), part), cols] = value[:, n].reshape(part, pair).astype(BF16)
            return 0

        lax.fori_loop(0, up_t.shape[0] // tile, step, 0)
        for c in (2 * g, 2 * g + 1):
            for df in range(1, fsdp):
                gx_copy(df, c).start()

    def merge(c):
        total = gw_out[f, :, head(c)].astype(F32)
        for df in range(1, fsdp):
            gx_came(df, c)
            total = total + gw_in[df, :, head(c)].astype(F32)
        for n in range(planes):
            zw_out[n, :, head(c)] = total[n * plane_rows : (n + 1) * plane_rows].astype(BF16)
        for dp in range(1, planes):
            gz_copy(dp, c).start()

    def total_up(c):
        total = zw_out[p, :, head(c)].astype(F32)
        for dp in range(1, planes):
            gz_came(dp, c)
            total = total + zw_in[dp, :, head(c)].astype(F32)
        for n in range(SPAN):
            fin_out[n, :, head(c)] = total[n * own_rows : (n + 1) * own_rows].astype(BF16)
        for d in (2, 3, 1):
            f_copy(d, c).start()

    def finish(c):
        for d in around:
            f_came(d, c)
        out_w[:, wide_head(r, c)] = fin_out[r, :, head(c)].astype(F32)
        for d in around:
            out_w[:, wide_head(peer[d], c)] = fin_in[peer[d], :, head(c)].astype(F32)

    forward(0)
    forward(1)
    for copy in own_copies:
        copy.wait()
    attend(0)
    attend(1)
    up_came(2)
    up_copy(3).start()
    up_came(1)
    up_came(3)
    for i in range(up_t.shape[0] // tile):
        up_t[i * tile : (i + 1) * tile, :] = up[:, i * tile : (i + 1) * tile].T
    weigh(0)
    project(0)
    backward(0)
    forward(2)
    backward(1)
    merge(0)
    forward(3)
    attend(2)
    project(1)
    collect(0)
    merge(1)
    attend(3)
    weigh(1)
    total_up(0)
    backward(2)
    collect(1)
    total_up(1)
    backward(3)
    merge(2)
    collect(2)
    merge(3)
    total_up(2)
    collect(3)
    total_up(3)
    for c in range(heads):
        finish(c)

    for c in range(heads):
        for d in around:
            dq_came(d, c)
            dk_came(d, c)
            for copy in (kv_copy(d, c), q_copy(d, c), dq_copy(d, c), dk_copy(d, c), f_copy(d, c)):
                copy.wait_send()
        own_dq(c).wait()
        own_dk(c).wait()
        for df in range(1, fsdp):
            w_copy(df, c).wait_send()
            gx_copy(df, c).wait_send()
        for dp in range(1, planes):
            gz_copy(dp, c).wait_send()

        @pl.when(not_last)
        def _(c=c):
            for d in range(SPAN):
                kz_copy(d, c).wait_send()

        @pl.when(not_first)
        def _(c=c):
            dz_copy(c).wait_send()

    for d in around:
        up_copy(d).wait_send()


def shards(queries, keys_values, upstream, out_weight):
    seqs, toks, width = queries.shape
    ctx, fsdp = lax.axis_size("ctx"), lax.axis_size("fsdp")
    planes = ctx // SPAN
    model = upstream.shape[2]
    own_rows = model // (ctx * fsdp)
    quarter = width // SPAN
    heads = quarter // HEAD_DIM
    group = SPAN * toks
    kv = jnp.swapaxes(keys_values[0], 0, 1)
    dma = pltpu.SemaphoreType.DMA
    any_spec = pl.BlockSpec(memory_space=pl.ANY)
    vm = pl.BlockSpec(memory_space=pltpu.VMEM)
    near = dma((SPAN, heads))
    line = dma((heads,))
    sides = dma((fsdp, heads))
    levels = dma((planes, heads))
    dq, out_kv, out_w = pl.pallas_call(
        functools.partial(layer_kernel, planes, fsdp),
        out_shape=(
            jax.ShapeDtypeStruct((toks, width), BF16),
            jax.ShapeDtypeStruct((2, toks, width), BF16),
            jax.ShapeDtypeStruct((own_rows, width), F32),
        ),
        in_specs=[any_spec] * 4,
        out_specs=(any_spec, any_spec, vm),
        scratch_shapes=[
            pltpu.VMEM((group, quarter), BF16),
            pltpu.VMEM((2, 2 * group, quarter), BF16),
            pltpu.VMEM((group, model), BF16),
            pltpu.VMEM((model, group), BF16),
            pltpu.VMEM((model, quarter), BF16),
            pltpu.VMEM((group, quarter), BF16),
            pltpu.VMEM((group, quarter), BF16),
            pltpu.VMEM((heads * SPAN, toks, group + toks), BF16),
            pltpu.VMEM((SPAN, toks, group + toks), F32),
            pltpu.VMEM((group, quarter), BF16),
            pltpu.VMEM((2, 2 * group, quarter), F32),
            pltpu.VMEM((2, group, quarter), BF16),
            pltpu.VMEM((2, group, quarter), BF16),
            pltpu.VMEM((2, group, quarter), BF16),
            pltpu.VMEM((fsdp, model // fsdp, quarter), BF16),
            pltpu.VMEM((fsdp, model // fsdp, quarter), BF16),
            pltpu.VMEM((planes, SPAN * own_rows, quarter), BF16),
            pltpu.VMEM((planes, SPAN * own_rows, quarter), BF16),
            pltpu.VMEM((SPAN, own_rows, quarter), BF16),
            pltpu.VMEM((SPAN, own_rows, quarter), BF16),
            dma((4,)), near, near, near, near, dma((SPAN,)), dma((SPAN,)), sides, sides, near, near,
            near, near, line, line, near, near, sides, sides, levels, levels, near, near,
        ],
        compiler_params=pltpu.CompilerParams(collective_id=0, has_side_effects=True),
        name="layer",
    )(queries[0], kv, upstream[0], out_weight)
    return dq[None], jnp.swapaxes(out_kv, 0, 1)[None], out_w


def solution(mesh):
    return jax.shard_map(
        shards,
        mesh=mesh,
        in_specs=(
            P("fsdp", "ctx", None),
            P("fsdp", "ctx", None, None),
            P("fsdp", "ctx", None),
            P("fsdp", None),
        ),
        out_specs=(P("fsdp", "ctx", None), P("fsdp", "ctx", None, None), P(("ctx", "fsdp"), None)),
        check_vma=False,
    )
```

```python
import functools

import jax
import jax.numpy as jnp
from jax import lax
from jax.experimental import pallas as pl
from jax.experimental.pallas import tpu as pltpu
from jax.sharding import PartitionSpec as P

HEAD_DIM = 128
SPAN = 4
NEGATIVE = -1e30
F32 = jnp.float32
BF16 = jnp.bfloat16
NT = (((1,), (1,)), ((), ()))
TN = (((0,), (0,)), ((), ()))


def remote(src, dst, send, recv, device):
    return pltpu.make_async_remote_copy(
        src_ref=src, dst_ref=dst, send_sem=send, recv_sem=recv, device_id=device, device_id_type=pl.DeviceIdType.MESH
    )


def layer_kernel(
    planes, fsdp,
    q_in, kv_in, up_in, weight,
    dq_out, kv_out, out_w,
    q, kv, up, up_t, w, ga, att, low, bias, dq, dkv, dprev, dprev_in, dsum,
    gw_out, gw_in, zw_out, pin, tin, fin_out, fin_in,
    own_sem, kv_s, kv_r, q_s, q_r, u_s, u_r, w_s, w_r, kz_s, kz_r,
    dq_s, dq_r, dz_s, dz_r, dk_s, dk_r, gx_s, gx_r, pin_s, pin_r, tin_s, tin_r, f_s, f_r,
):
    toks = q_in.shape[0]
    depth = weight.shape[0]
    width = weight.shape[1]
    quarter = width // SPAN
    heads = quarter // HEAD_DIM
    plane_toks = SPAN * toks
    keys = plane_toks + toks
    own_rows = out_w.shape[0]
    plane_rows = SPAN * own_rows
    inv_root = HEAD_DIM ** (-0.5)

    me = lax.axis_index("ctx")
    f = lax.axis_index("fsdp")
    p = lax.div(me, SPAN)
    r = lax.rem(me, SPAN)
    mate = r + 1 - 2 * lax.rem(r, 2)
    peer = [r, mate, lax.rem(r + 2, SPAN), lax.rem(mate + 2, SPAN)]
    not_first = p > 0
    not_last = p < planes - 1

    def dev(p_, r_, f_):
        return {"ctx": p_ * SPAN + r_, "fsdp": f_}

    def near(d):
        return dev(p, peer[d], f)

    def side(df):
        return lax.rem(f + df, fsdp)

    def level(dp):
        return lax.rem(p + dp, planes)

    def rows(i):
        return pl.ds(pl.multiple_of(i * toks, toks), toks)

    def own_plane(i):
        return pl.ds(pl.multiple_of(plane_toks + i * toks, toks), toks)

    def head(c):
        return pl.ds(c * HEAD_DIM, HEAD_DIM)

    def wide_head(i, c):
        return pl.ds(pl.multiple_of(i * quarter + c * HEAD_DIM, HEAD_DIM), HEAD_DIM)

    def quart(i):
        return pl.ds(pl.multiple_of(i * quarter, quarter), quarter)

    def w_rows(i):
        return pl.ds(pl.multiple_of(i * depth, depth), depth)

    own_copies = [
        pltpu.make_async_copy(kv_in.at[:, :, quart(r)], kv.at[:, own_plane(r), :], own_sem.at[0]),
        pltpu.make_async_copy(q_in.at[:, quart(r)], q.at[rows(r), :], own_sem.at[1]),
        pltpu.make_async_copy(up_in, up.at[rows(r), :], own_sem.at[2]),
        pltpu.make_async_copy(weight.at[:, quart(r)], w.at[w_rows(f), :], own_sem.at[3]),
    ]
    for copy in own_copies:
        copy.start()

    sem = pltpu.get_barrier_semaphore()
    targets = [near(d) for d in range(1, SPAN)]
    targets += [dev(p, r, side(df)) for df in range(1, fsdp)]
    targets += [dev(level(dp), r, f) for dp in range(1, planes)]
    for target in targets:
        pl.semaphore_signal(sem, inc=1, device_id=target, device_id_type=pl.DeviceIdType.MESH)
    pl.semaphore_wait(sem, len(targets))

    def kv_copy(d, c):
        return remote(kv_in.at[:, :, wide_head(peer[d], c)], kv.at[:, own_plane(r), head(c)], kv_s.at[d, c], kv_r.at[d, c], near(d))

    def kv_came(d, c):
        here = kv.at[:, own_plane(peer[d]), head(c)]
        remote(here, here, kv_s.at[d, c], kv_r.at[d, c], near(d)).wait_recv()

    def q_copy(d, c):
        return remote(q_in.at[:, wide_head(peer[d], c)], q.at[rows(r), head(c)], q_s.at[d, c], q_r.at[d, c], near(d))

    def q_came(d, c):
        here = q.at[rows(peer[d]), head(c)]
        remote(here, here, q_s.at[d, c], q_r.at[d, c], near(d)).wait_recv()

    def up_copy(d):
        if d == 3:
            here = up.at[rows(peer[2]), :]
            return remote(here, here, u_s.at[3], u_r.at[3], near(1))
        return remote(up_in, up.at[rows(r), :], u_s.at[d], u_r.at[d], near(d))

    def up_came(d):
        here = up.at[rows(peer[d]), :]
        remote(here, here, u_s.at[d], u_r.at[d], near(d)).wait_recv()

    def w_copy(df, c):
        return remote(
            weight.at[:, wide_head(r, c)], w.at[w_rows(f), head(c)], w_s.at[df, c], w_r.at[fsdp - df, c], dev(p, r, side(df))
        )

    def w_came(df, c):
        here = w.at[w_rows(side(df)), head(c)]
        remote(here, here, w_s.at[df, c], w_r.at[df, c], dev(p, r, side(df))).wait_recv()

    def kz_copy(d, c):
        src = kv_in.at[:, :, wide_head(r, c)] if d == 0 else kv.at[:, own_plane(peer[d]), head(c)]
        return remote(src, kv.at[:, rows(peer[d]), head(c)], kz_s.at[d, c], kz_r.at[d, c], dev(p + 1, r, f))

    def dq_copy(d, c):
        return remote(dq.at[rows(peer[d]), head(c)], dq_out.at[:, wide_head(r, c)], dq_s.at[d, c], dq_r.at[d, c], near(d))

    def dq_came(d, c):
        here = dq_out.at[:, wide_head(peer[d], c)]
        remote(here, here, dq_s.at[d, c], dq_r.at[d, c], near(d)).wait_recv()

    def own_dq(c):
        return pltpu.make_async_copy(dq.at[rows(r), head(c)], dq_out.at[:, wide_head(r, c)], dq_s.at[0, c])

    def dz_copy(c):
        return remote(dprev.at[:, :, head(c)], dprev_in.at[:, :, head(c)], dz_s.at[c], dz_r.at[c], dev(p - 1, r, f))

    def dk_copy(d, c):
        return remote(dsum.at[:, rows(peer[d]), head(c)], kv_out.at[:, :, wide_head(r, c)], dk_s.at[d, c], dk_r.at[d, c], near(d))

    def dk_came(d, c):
        here = kv_out.at[:, :, wide_head(peer[d], c)]
        remote(here, here, dk_s.at[d, c], dk_r.at[d, c], near(d)).wait_recv()

    def own_dk(c):
        return pltpu.make_async_copy(dsum.at[:, rows(r), head(c)], kv_out.at[:, :, wide_head(r, c)], dk_s.at[0, c])

    def gx_copy(df, c):
        return remote(
            gw_out.at[side(df), :, head(c)], gw_in.at[fsdp - df, :, head(c)], gx_s.at[df, c], gx_r.at[fsdp - df, c],
            dev(p, r, side(df)),
        )

    def gx_came(df, c):
        here = gw_in.at[df, :, head(c)]
        remote(here, here, gx_s.at[df, c], gx_r.at[df, c], dev(p, r, side(df))).wait_recv()

    lower = lax.rem(p, 2) == 0
    partner = dev(p + 1 - 2 * lax.rem(p, 2), r, f)
    group = lax.div(p, 2)

    def to_partner(n):
        return jnp.logical_or(jnp.logical_and(lower, n > p), jnp.logical_and(jnp.logical_not(lower), n < p))

    def to_plane(n):
        return jnp.logical_or(jnp.logical_and(lower, n < p), jnp.logical_and(jnp.logical_not(lower), n > p))

    def pin_copy(n, c):
        return remote(zw_out.at[n, :, head(c)], pin.at[n, :, head(c)], pin_s.at[n, c], pin_r.at[n, c], partner)

    def tin_copy(n, c):
        return remote(zw_out.at[n, :, head(c)], tin.at[group, :, head(c)], tin_s.at[n, c], tin_r.at[group, c], dev(n, r, f))

    def tin_came(k, c):
        here = tin.at[k, :, head(c)]
        remote(here, here, tin_s.at[0, c], tin_r.at[k, c], partner).wait_recv()

    def f_copy(d, c):
        return remote(fin_out.at[peer[d], :, head(c)], fin_in.at[r, :, head(c)], f_s.at[d, c], f_r.at[d, c], near(d))

    def f_came(d, c):
        here = fin_in.at[peer[d], :, head(c)]
        remote(here, here, f_s.at[d, c], f_r.at[d, c], near(d)).wait_recv()

    around = range(1, SPAN)

    def spread(c):
        for d in around:
            kv_copy(d, c).start()
        for d in around:
            q_copy(d, c).start()

    def halo(c):
        @pl.when(not_last)
        def _():
            kz_copy(0, c).start()

    def columns(c):
        for df in range(1, fsdp):
            w_copy(df, c).start()

    def lift():
        up_copy(2).start()
        up_copy(1).start()

    spread(0)
    lift()
    columns(1)
    spread(2)
    spread(3)
    columns(0)
    columns(2)
    columns(3)
    halo(1)
    halo(0)
    spread(1)
    halo(3)
    halo(2)
    row = lax.broadcasted_iota(jnp.int32, (toks, keys), 0)
    col = lax.broadcasted_iota(jnp.int32, (toks, keys), 1)
    for b in range(SPAN):
        first = jnp.where(not_first, 0, plane_toks - b * toks)
        bias[b] = jnp.where((col > row) & (col <= row + plane_toks) & (col >= first), 0.0, NEGATIVE)
    dkv[...] = jnp.zeros(dkv.shape, F32)

    @pl.when(p == 0)
    def _():
        kv[:, :plane_toks] = jnp.zeros((2, plane_toks, quarter), BF16)

    def forward(c):
        for d in around:
            kv_came(d, c)

            @pl.when(not_last)
            def _(d=d):
                kz_copy(d, c).start()

    def window(b):
        return pl.ds(b * toks, keys)

    def attend(c):
        for d in around:
            q_came(d, c)

        @pl.when(not_first)
        def _():
            for d in range(SPAN):
                here = kv.at[:, rows(peer[d]), head(c)]
                remote(here, here, kz_s.at[d, c], kz_r.at[d, c], near(1)).wait_recv()

        for b in range(SPAN):
            block = pl.ds(b * toks, toks)
            scores = lax.dot_general(q[block, head(c)], kv[0, window(b), head(c)], NT, preferred_element_type=F32) * inv_root + bias[b]
            lifted = jnp.exp(scores - jnp.max(scores, axis=-1, keepdims=True))
            prob = (lifted * (1.0 / jnp.sum(lifted, axis=-1, keepdims=True))).astype(BF16)
            low[c * SPAN + b] = prob
            att[block, head(c)] = jnp.dot(prob, kv[1, window(b), head(c)], preferred_element_type=F32).astype(BF16)

    def backward(c):
        for b in range(SPAN):
            block = pl.ds(b * toks, toks)
            g = ga[block, head(c)]
            prob = low[c * SPAN + b]
            k = kv[0, window(b), head(c)]
            products = lax.dot_general(g, kv[1, window(b), head(c)], NT, preferred_element_type=F32)
            center = jnp.sum(g.astype(F32) * att[block, head(c)].astype(F32), axis=-1, keepdims=True)
            ds = (prob.astype(F32) * (products - center)).astype(BF16)
            dq[block, head(c)] = (jnp.dot(ds, k, preferred_element_type=F32) * inv_root).astype(BF16)
            dkv[0, window(b), head(c)] += lax.dot_general(ds, q[block, head(c)], TN, preferred_element_type=F32) * inv_root
            dkv[1, window(b), head(c)] += lax.dot_general(prob, g, TN, preferred_element_type=F32)
        for d in (2, 3, 1):
            dq_copy(d, c).start()
        own_dq(c).start()
        dprev[:, :, head(c)] = dkv[:, :plane_toks, head(c)].astype(BF16)

        @pl.when(not_first)
        def _():
            dz_copy(c).start()

    def collect(c):
        @pl.when(not_last)
        def _():
            dz_copy(c).wait_recv()
            dsum[:, :, head(c)] = (dkv[:, plane_toks:, head(c)] + dprev_in[:, :, head(c)].astype(F32)).astype(BF16)

        @pl.when(p == planes - 1)
        def _():
            dsum[:, :, head(c)] = dkv[:, plane_toks:, head(c)].astype(BF16)

        for d in (2, 3, 1):
            dk_copy(d, c).start()
        own_dk(c).start()

    def project(c, d):
        if d == 0:
            for df in range(1, fsdp):
                w_came(df, c)
        ga[rows(peer[d]), head(c)] = jnp.dot(up[rows(peer[d]), :], w[:, head(c)], preferred_element_type=F32).astype(BF16)

    def turn(d):
        up_t[:, rows(peer[d])] = up[rows(peer[d]), :].T

    tile = plane_toks
    unit = fsdp * own_rows

    def weigh(c):
        def step(t, _):
            value = jnp.dot(up_t[pl.ds(pl.multiple_of(t * tile, tile), tile), :], att[:, head(c)], preferred_element_type=F32)
            value = value.reshape(tile // unit, fsdp, own_rows, HEAD_DIM)
            part = tile // fsdp
            for n in range(fsdp):
                gw_out[n, pl.ds(pl.multiple_of(t * part, part), part), head(c)] = value[:, n].reshape(part, HEAD_DIM).astype(BF16)
            return 0

        lax.fori_loop(0, up_t.shape[0] // tile, step, 0)
        for df in range(1, fsdp):
            gx_copy(df, c).start()

    def merge(c):
        total = gw_out[f, :, head(c)].astype(F32)
        for df in range(1, fsdp):
            gx_came(df, c)
            total = total + gw_in[df, :, head(c)].astype(F32)
        for n in range(planes):
            zw_out[n, :, head(c)] = total[n * plane_rows : (n + 1) * plane_rows].astype(BF16)
        for n in range(planes):
            @pl.when(to_partner(n))
            def _(n=n):
                pin_copy(n, c).start()

    def relay(c):
        for n in range(planes):
            @pl.when(to_plane(n))
            def _(n=n):
                pin_copy(n, c).wait_recv()
                zw_out[n, :, head(c)] = (zw_out[n, :, head(c)].astype(F32) + pin[n, :, head(c)].astype(F32)).astype(BF16)
                tin_copy(n, c).start()

    def total_up(c):
        pin_copy(p, c).wait_recv()
        total = zw_out[p, :, head(c)].astype(F32) + pin[p, :, head(c)].astype(F32)
        for dk in range(1, planes // 2):
            k = lax.rem(group + dk, planes // 2)
            tin_came(k, c)
            total = total + tin[k, :, head(c)].astype(F32)
        for n in range(SPAN):
            fin_out[n, :, head(c)] = total[n * own_rows : (n + 1) * own_rows].astype(BF16)
        for d in (2, 3, 1):
            f_copy(d, c).start()

    def finish(c):
        for d in around:
            f_came(d, c)
        out_w[:, wide_head(r, c)] = fin_out[r, :, head(c)].astype(F32)
        for d in around:
            out_w[:, wide_head(peer[d], c)] = fin_in[peer[d], :, head(c)].astype(F32)

    def settle():
        for copy in own_copies:
            copy.wait()
        up_came(1)
        turn(0)
        turn(1)

    def lift_on():
        up_came(2)
        up_copy(3).start()
        turn(2)

    def lift_end():
        up_came(3)
        turn(3)

    def project_chip(c):
        project(c, 0)
        project(c, 1)

    def project_rest(c):
        project(c, 2)
        project(c, 3)

    settle()
    forward(0)
    project_chip(0)
    lift_on()
    attend(0)
    lift_end()
    project_rest(0)
    forward(2)
    project_chip(1)
    backward(0)
    weigh(0)
    project_rest(1)
    project_chip(2)
    project_rest(2)
    forward(3)
    attend(2)
    backward(2)
    weigh(2)
    project_chip(3)
    project_rest(3)
    forward(1)
    collect(0)
    merge(0)
    attend(3)
    weigh(3)
    attend(1)
    relay(0)
    merge(2)
    weigh(1)
    backward(3)
    relay(2)
    merge(1)
    total_up(0)
    collect(2)
    total_up(2)
    relay(1)
    merge(3)
    backward(1)
    relay(3)
    total_up(1)
    collect(3)
    finish(0)
    collect(1)
    finish(1)
    finish(2)
    total_up(3)
    finish(3)
    for c in range(heads):
        for d in around:
            dq_came(d, c)
            dk_came(d, c)
            for copy in (kv_copy(d, c), q_copy(d, c), dq_copy(d, c), dk_copy(d, c), f_copy(d, c)):
                copy.wait_send()
        own_dq(c).wait()
        own_dk(c).wait()
        for df in range(1, fsdp):
            w_copy(df, c).wait_send()
            gx_copy(df, c).wait_send()
        for n in range(planes):
            @pl.when(to_partner(n))
            def _(n=n, c=c):
                pin_copy(n, c).wait_send()

            @pl.when(to_plane(n))
            def _(n=n, c=c):
                tin_copy(n, c).wait_send()

        @pl.when(not_last)
        def _(c=c):
            for d in range(SPAN):
                kz_copy(d, c).wait_send()

        @pl.when(not_first)
        def _(c=c):
            dz_copy(c).wait_send()

    for d in around:
        up_copy(d).wait_send()


def shards(queries, keys_values, upstream, out_weight):
    seqs, toks, width = queries.shape
    ctx, fsdp = lax.axis_size("ctx"), lax.axis_size("fsdp")
    planes = ctx // SPAN
    model = upstream.shape[2]
    own_rows = model // (ctx * fsdp)
    quarter = width // SPAN
    heads = quarter // HEAD_DIM
    group = SPAN * toks
    kv = jnp.swapaxes(keys_values[0], 0, 1)
    dma = pltpu.SemaphoreType.DMA
    any_spec = pl.BlockSpec(memory_space=pl.ANY)
    vm = pl.BlockSpec(memory_space=pltpu.VMEM)
    near = dma((SPAN, heads))
    line = dma((heads,))
    sides = dma((fsdp, heads))
    levels = dma((planes, heads))
    dq, out_kv, out_w = pl.pallas_call(
        functools.partial(layer_kernel, planes, fsdp),
        out_shape=(
            jax.ShapeDtypeStruct((toks, width), BF16),
            jax.ShapeDtypeStruct((2, toks, width), BF16),
            jax.ShapeDtypeStruct((own_rows, width), F32),
        ),
        in_specs=[any_spec] * 4,
        out_specs=(any_spec, any_spec, vm),
        scratch_shapes=[
            pltpu.VMEM((group, quarter), BF16),
            pltpu.VMEM((2, 2 * group, quarter), BF16),
            pltpu.VMEM((group, model), BF16),
            pltpu.VMEM((model, group), BF16),
            pltpu.VMEM((model, quarter), BF16),
            pltpu.VMEM((group, quarter), BF16),
            pltpu.VMEM((group, quarter), BF16),
            pltpu.VMEM((heads * SPAN, toks, group + toks), BF16),
            pltpu.VMEM((SPAN, toks, group + toks), F32),
            pltpu.VMEM((group, quarter), BF16),
            pltpu.VMEM((2, 2 * group, quarter), F32),
            pltpu.VMEM((2, group, quarter), BF16),
            pltpu.VMEM((2, group, quarter), BF16),
            pltpu.VMEM((2, group, quarter), BF16),
            pltpu.VMEM((fsdp, model // fsdp, quarter), BF16),
            pltpu.VMEM((fsdp, model // fsdp, quarter), BF16),
            pltpu.VMEM((planes, SPAN * own_rows, quarter), BF16),
            pltpu.VMEM((planes, SPAN * own_rows, quarter), BF16),
            pltpu.VMEM((planes // 2, SPAN * own_rows, quarter), BF16),
            pltpu.VMEM((SPAN, own_rows, quarter), BF16),
            pltpu.VMEM((SPAN, own_rows, quarter), BF16),
            dma((4,)), near, near, near, near, dma((SPAN,)), dma((SPAN,)), sides, sides, near, near,
            near, near, line, line, near, near, sides, sides, levels, levels, levels, dma((planes // 2, heads)), near, near,
        ],
        compiler_params=pltpu.CompilerParams(collective_id=0, has_side_effects=True),
        name="layer",
    )(queries[0], kv, upstream[0], out_weight)
    return dq[None], jnp.swapaxes(out_kv, 0, 1)[None], out_w


def solution(mesh):
    return jax.shard_map(
        shards,
        mesh=mesh,
        in_specs=(
            P("fsdp", "ctx", None),
            P("fsdp", "ctx", None, None),
            P("fsdp", "ctx", None),
            P("fsdp", None),
        ),
        out_specs=(P("fsdp", "ctx", None), P("fsdp", "ctx", None, None), P(("ctx", "fsdp"), None)),
        check_vma=False,
    )
```

```python
import functools

import jax
import jax.numpy as jnp
from jax import lax
from jax.experimental import pallas as pl
from jax.experimental.pallas import tpu as pltpu
from jax.sharding import PartitionSpec as P

HEAD_DIM = 128
SPAN = 4
NEGATIVE = -1e30
F32 = jnp.float32
BF16 = jnp.bfloat16
NT = (((1,), (1,)), ((), ()))
TN = (((0,), (0,)), ((), ()))


def remote(src, dst, send, recv, device):
    return pltpu.make_async_remote_copy(
        src_ref=src, dst_ref=dst, send_sem=send, recv_sem=recv, device_id=device, device_id_type=pl.DeviceIdType.MESH
    )


def layer_kernel(
    planes, fsdp,
    q_in, kv_pairs, up_in, weight,
    dq_out, kv_out, out_w,
    kv_raw, kv_in, q, kv, up, up_t, w, ga, att, low, bias, dq, dkv, dprev, dprev_in, dsum,
    gw_out, gw_in, zw_out, pin, tin, fin_out, fin_in,
    own_sem, kv_s, kv_r, q_s, q_r, u_s, u_r, w_s, w_r, kz_s, kz_r,
    dq_s, dq_r, dz_s, dz_r, dk_s, dk_r, gx_s, gx_r, pin_s, pin_r, tin_s, tin_r, f_s, f_r,
):
    toks = q_in.shape[0]
    depth = weight.shape[0]
    width = weight.shape[1]
    quarter = width // SPAN
    heads = quarter // HEAD_DIM
    plane_toks = SPAN * toks
    keys = plane_toks + toks
    own_rows = out_w.shape[0]
    plane_rows = SPAN * own_rows
    inv_root = HEAD_DIM ** (-0.5)

    me = lax.axis_index("ctx")
    f = lax.axis_index("fsdp")
    p = lax.div(me, SPAN)
    r = lax.rem(me, SPAN)
    mate = r + 1 - 2 * lax.rem(r, 2)
    peer = [r, mate, lax.rem(r + 2, SPAN), lax.rem(mate + 2, SPAN)]
    not_first = p > 0
    not_last = p < planes - 1

    def dev(p_, r_, f_):
        return {"ctx": p_ * SPAN + r_, "fsdp": f_}

    def near(d):
        return dev(p, peer[d], f)

    def side(df):
        return lax.rem(f + df, fsdp)

    def level(dp):
        return lax.rem(p + dp, planes)

    def rows(i):
        return pl.ds(pl.multiple_of(i * toks, toks), toks)

    def own_plane(i):
        return pl.ds(pl.multiple_of(plane_toks + i * toks, toks), toks)

    def head(c):
        return pl.ds(c * HEAD_DIM, HEAD_DIM)

    def wide_head(i, c):
        return pl.ds(pl.multiple_of(i * quarter + c * HEAD_DIM, HEAD_DIM), HEAD_DIM)

    def quart(i):
        return pl.ds(pl.multiple_of(i * quarter, quarter), quarter)

    def w_rows(i):
        return pl.ds(pl.multiple_of(i * depth, depth), depth)

    pairs_copy = pltpu.make_async_copy(kv_pairs, kv_raw, own_sem.at[0])
    pairs_copy.start()
    own_copies = [
        pltpu.make_async_copy(q_in.at[:, quart(r)], q.at[rows(r), :], own_sem.at[1]),
        pltpu.make_async_copy(up_in, up.at[rows(r), :], own_sem.at[2]),
        pltpu.make_async_copy(weight.at[:, quart(r)], w.at[w_rows(f), :], own_sem.at[3]),
    ]
    for copy in own_copies:
        copy.start()

    sem = pltpu.get_barrier_semaphore()
    targets = [near(d) for d in range(1, SPAN)]
    targets += [dev(p, r, side(df)) for df in range(1, fsdp)]
    targets += [dev(level(dp), r, f) for dp in range(1, planes)]
    for target in targets:
        pl.semaphore_signal(sem, inc=1, device_id=target, device_id_type=pl.DeviceIdType.MESH)
    pairs_copy.wait()
    for n in range(2):
        kv_in[n] = kv_raw[:, n, :]
    pl.semaphore_wait(sem, len(targets))

    def kv_copy(d, c):
        return remote(kv_in.at[:, :, wide_head(peer[d], c)], kv.at[:, own_plane(r), head(c)], kv_s.at[d, c], kv_r.at[d, c], near(d))

    def kv_came(d, c):
        here = kv.at[:, own_plane(peer[d]), head(c)]
        remote(here, here, kv_s.at[d, c], kv_r.at[d, c], near(d)).wait_recv()

    def q_copy(d, c):
        return remote(q_in.at[:, wide_head(peer[d], c)], q.at[rows(r), head(c)], q_s.at[d, c], q_r.at[d, c], near(d))

    def q_came(d, c):
        here = q.at[rows(peer[d]), head(c)]
        remote(here, here, q_s.at[d, c], q_r.at[d, c], near(d)).wait_recv()

    def up_copy(d):
        if d == 3:
            here = up.at[rows(peer[2]), :]
            return remote(here, here, u_s.at[3], u_r.at[3], near(1))
        return remote(up_in, up.at[rows(r), :], u_s.at[d], u_r.at[d], near(d))

    def up_came(d):
        here = up.at[rows(peer[d]), :]
        remote(here, here, u_s.at[d], u_r.at[d], near(d)).wait_recv()

    def w_copy(df, c):
        return remote(
            weight.at[:, wide_head(r, c)], w.at[w_rows(f), head(c)], w_s.at[df, c], w_r.at[fsdp - df, c], dev(p, r, side(df))
        )

    def w_came(df, c):
        here = w.at[w_rows(side(df)), head(c)]
        remote(here, here, w_s.at[df, c], w_r.at[df, c], dev(p, r, side(df))).wait_recv()

    def kz_copy(d, c):
        src = kv_in.at[:, :, wide_head(r, c)] if d == 0 else kv.at[:, own_plane(peer[d]), head(c)]
        return remote(src, kv.at[:, rows(peer[d]), head(c)], kz_s.at[d, c], kz_r.at[d, c], dev(p + 1, r, f))

    def dq_copy(d, c):
        return remote(dq.at[rows(peer[d]), head(c)], dq_out.at[:, wide_head(r, c)], dq_s.at[d, c], dq_r.at[d, c], near(d))

    def dq_came(d, c):
        here = dq_out.at[:, wide_head(peer[d], c)]
        remote(here, here, dq_s.at[d, c], dq_r.at[d, c], near(d)).wait_recv()

    def own_dq(c):
        return pltpu.make_async_copy(dq.at[rows(r), head(c)], dq_out.at[:, wide_head(r, c)], dq_s.at[0, c])

    def dz_copy(c):
        return remote(dprev.at[:, :, head(c)], dprev_in.at[:, :, head(c)], dz_s.at[c], dz_r.at[c], dev(p - 1, r, f))

    def dk_copy(d, c):
        return remote(dsum.at[:, rows(peer[d]), head(c)], kv_out.at[:, :, wide_head(r, c)], dk_s.at[d, c], dk_r.at[d, c], near(d))

    def dk_came(d, c):
        here = kv_out.at[:, :, wide_head(peer[d], c)]
        remote(here, here, dk_s.at[d, c], dk_r.at[d, c], near(d)).wait_recv()

    def own_dk(c):
        return pltpu.make_async_copy(dsum.at[:, rows(r), head(c)], kv_out.at[:, :, wide_head(r, c)], dk_s.at[0, c])

    def gx_copy(df, c):
        return remote(
            gw_out.at[side(df), :, head(c)], gw_in.at[fsdp - df, :, head(c)], gx_s.at[df, c], gx_r.at[fsdp - df, c],
            dev(p, r, side(df)),
        )

    def gx_came(df, c):
        here = gw_in.at[df, :, head(c)]
        remote(here, here, gx_s.at[df, c], gx_r.at[df, c], dev(p, r, side(df))).wait_recv()

    lower = lax.rem(p, 2) == 0
    partner = dev(p + 1 - 2 * lax.rem(p, 2), r, f)
    group = lax.div(p, 2)

    def to_partner(n):
        return jnp.logical_or(jnp.logical_and(lower, n > p), jnp.logical_and(jnp.logical_not(lower), n < p))

    def to_plane(n):
        return jnp.logical_or(jnp.logical_and(lower, n < p), jnp.logical_and(jnp.logical_not(lower), n > p))

    def pin_copy(n, c):
        return remote(zw_out.at[n, :, head(c)], pin.at[n, :, head(c)], pin_s.at[n, c], pin_r.at[n, c], partner)

    def tin_copy(n, c):
        return remote(zw_out.at[n, :, head(c)], tin.at[group, :, head(c)], tin_s.at[n, c], tin_r.at[group, c], dev(n, r, f))

    def tin_came(k, c):
        here = tin.at[k, :, head(c)]
        remote(here, here, tin_s.at[0, c], tin_r.at[k, c], partner).wait_recv()

    def f_copy(d, c):
        return remote(fin_out.at[peer[d], :, head(c)], fin_in.at[r, :, head(c)], f_s.at[d, c], f_r.at[d, c], near(d))

    def f_came(d, c):
        here = fin_in.at[peer[d], :, head(c)]
        remote(here, here, f_s.at[d, c], f_r.at[d, c], near(d)).wait_recv()

    around = range(1, SPAN)

    def spread(c):
        for d in around:
            kv_copy(d, c).start()
        for d in around:
            q_copy(d, c).start()

    def halo(c):
        @pl.when(not_last)
        def _():
            kz_copy(0, c).start()

    def columns(c):
        for df in range(1, fsdp):
            w_copy(df, c).start()

    def lift():
        up_copy(2).start()
        up_copy(1).start()

    spread(0)
    lift()
    columns(1)
    spread(2)
    spread(3)
    columns(0)
    columns(2)
    columns(3)
    halo(1)
    halo(0)
    spread(1)
    halo(3)
    halo(2)
    row = lax.broadcasted_iota(jnp.int32, (toks, keys), 0)
    col = lax.broadcasted_iota(jnp.int32, (toks, keys), 1)
    for b in range(SPAN):
        first = jnp.where(not_first, 0, plane_toks - b * toks)
        bias[b] = jnp.where((col > row) & (col <= row + plane_toks) & (col >= first), 0.0, NEGATIVE)
    dkv[...] = jnp.zeros(dkv.shape, F32)

    @pl.when(p == 0)
    def _():
        kv[:, :plane_toks] = jnp.zeros((2, plane_toks, quarter), BF16)

    def forward(c):
        for d in around:
            kv_came(d, c)

            @pl.when(not_last)
            def _(d=d):
                kz_copy(d, c).start()

    def window(b):
        return pl.ds(b * toks, keys)

    def attend(c):
        for d in around:
            q_came(d, c)

        @pl.when(not_first)
        def _():
            for d in range(SPAN):
                here = kv.at[:, rows(peer[d]), head(c)]
                remote(here, here, kz_s.at[d, c], kz_r.at[d, c], near(1)).wait_recv()

        for b in range(SPAN):
            block = pl.ds(b * toks, toks)
            scores = lax.dot_general(q[block, head(c)], kv[0, window(b), head(c)], NT, preferred_element_type=F32) * inv_root + bias[b]
            lifted = jnp.exp(scores - jnp.max(scores, axis=-1, keepdims=True))
            prob = (lifted * (1.0 / jnp.sum(lifted, axis=-1, keepdims=True))).astype(BF16)
            low[c * SPAN + b] = prob
            att[block, head(c)] = jnp.dot(prob, kv[1, window(b), head(c)], preferred_element_type=F32).astype(BF16)

    def backward(c):
        for b in range(SPAN):
            block = pl.ds(b * toks, toks)
            g = ga[block, head(c)]
            prob = low[c * SPAN + b]
            k = kv[0, window(b), head(c)]
            products = lax.dot_general(g, kv[1, window(b), head(c)], NT, preferred_element_type=F32)
            center = jnp.sum(g.astype(F32) * att[block, head(c)].astype(F32), axis=-1, keepdims=True)
            ds = (prob.astype(F32) * (products - center)).astype(BF16)
            dq[block, head(c)] = (jnp.dot(ds, k, preferred_element_type=F32) * inv_root).astype(BF16)
            dkv[0, window(b), head(c)] += lax.dot_general(ds, q[block, head(c)], TN, preferred_element_type=F32) * inv_root
            dkv[1, window(b), head(c)] += lax.dot_general(prob, g, TN, preferred_element_type=F32)
        for d in (2, 3, 1):
            dq_copy(d, c).start()
        own_dq(c).start()
        dprev[:, :, head(c)] = dkv[:, :plane_toks, head(c)].astype(BF16)

        @pl.when(not_first)
        def _():
            dz_copy(c).start()

    def collect(c):
        @pl.when(not_last)
        def _():
            dz_copy(c).wait_recv()
            dsum[:, :, head(c)] = (dkv[:, plane_toks:, head(c)] + dprev_in[:, :, head(c)].astype(F32)).astype(BF16)

        @pl.when(p == planes - 1)
        def _():
            dsum[:, :, head(c)] = dkv[:, plane_toks:, head(c)].astype(BF16)

        for d in (2, 3, 1):
            dk_copy(d, c).start()
        own_dk(c).start()

    def project(c, d):
        if d == 0:
            for df in range(1, fsdp):
                w_came(df, c)
        ga[rows(peer[d]), head(c)] = jnp.dot(up[rows(peer[d]), :], w[:, head(c)], preferred_element_type=F32).astype(BF16)

    def turn(d):
        up_t[:, rows(peer[d])] = up[rows(peer[d]), :].T

    tile = plane_toks
    unit = fsdp * own_rows

    def weigh(c):
        def step(t, _):
            value = jnp.dot(up_t[pl.ds(pl.multiple_of(t * tile, tile), tile), :], att[:, head(c)], preferred_element_type=F32)
            value = value.reshape(tile // unit, fsdp, own_rows, HEAD_DIM)
            part = tile // fsdp
            for n in range(fsdp):
                gw_out[n, pl.ds(pl.multiple_of(t * part, part), part), head(c)] = value[:, n].reshape(part, HEAD_DIM).astype(BF16)
            return 0

        lax.fori_loop(0, up_t.shape[0] // tile, step, 0)
        for df in range(1, fsdp):
            gx_copy(df, c).start()

    def merge(c):
        total = gw_out[f, :, head(c)].astype(F32)
        for df in range(1, fsdp):
            gx_came(df, c)
            total = total + gw_in[df, :, head(c)].astype(F32)
        for n in range(planes):
            zw_out[n, :, head(c)] = total[n * plane_rows : (n + 1) * plane_rows].astype(BF16)
        for n in range(planes):
            @pl.when(to_partner(n))
            def _(n=n):
                pin_copy(n, c).start()

    def relay(c):
        for n in range(planes):
            @pl.when(to_plane(n))
            def _(n=n):
                pin_copy(n, c).wait_recv()
                zw_out[n, :, head(c)] = (zw_out[n, :, head(c)].astype(F32) + pin[n, :, head(c)].astype(F32)).astype(BF16)
                tin_copy(n, c).start()

    def total_up(c):
        pin_copy(p, c).wait_recv()
        total = zw_out[p, :, head(c)].astype(F32) + pin[p, :, head(c)].astype(F32)
        for dk in range(1, planes // 2):
            k = lax.rem(group + dk, planes // 2)
            tin_came(k, c)
            total = total + tin[k, :, head(c)].astype(F32)
        for n in range(SPAN):
            fin_out[n, :, head(c)] = total[n * own_rows : (n + 1) * own_rows].astype(BF16)
        for d in (2, 3, 1):
            f_copy(d, c).start()

    def finish(c):
        for d in around:
            f_came(d, c)
        out_w[:, wide_head(r, c)] = fin_out[r, :, head(c)].astype(F32)
        for d in around:
            out_w[:, wide_head(peer[d], c)] = fin_in[peer[d], :, head(c)].astype(F32)

    def settle():
        kv[:, own_plane(r), :] = kv_in[:, :, quart(r)]
        for copy in own_copies:
            copy.wait()
        up_came(1)
        turn(0)
        turn(1)

    def lift_on():
        up_came(2)
        up_copy(3).start()
        turn(2)

    def lift_end():
        up_came(3)
        turn(3)

    def project_chip(c):
        project(c, 0)
        project(c, 1)

    def project_rest(c):
        project(c, 2)
        project(c, 3)

    settle()
    forward(0)
    project_chip(0)
    lift_on()
    attend(0)
    lift_end()
    project_rest(0)
    forward(2)
    project_chip(1)
    backward(0)
    weigh(0)
    project_rest(1)
    project_chip(2)
    project_rest(2)
    forward(3)
    attend(2)
    backward(2)
    weigh(2)
    project_chip(3)
    project_rest(3)
    forward(1)
    collect(0)
    merge(0)
    attend(3)
    weigh(3)
    attend(1)
    relay(0)
    merge(2)
    weigh(1)
    backward(3)
    relay(2)
    merge(1)
    total_up(0)
    collect(2)
    total_up(2)
    relay(1)
    merge(3)
    backward(1)
    relay(3)
    total_up(1)
    collect(3)
    finish(0)
    collect(1)
    finish(1)
    finish(2)
    total_up(3)
    finish(3)
    for c in range(heads):
        for d in around:
            dq_came(d, c)
            dk_came(d, c)
            for copy in (kv_copy(d, c), q_copy(d, c), dq_copy(d, c), dk_copy(d, c), f_copy(d, c)):
                copy.wait_send()
        own_dq(c).wait()
        own_dk(c).wait()
        for df in range(1, fsdp):
            w_copy(df, c).wait_send()
            gx_copy(df, c).wait_send()
        for n in range(planes):
            @pl.when(to_partner(n))
            def _(n=n, c=c):
                pin_copy(n, c).wait_send()

            @pl.when(to_plane(n))
            def _(n=n, c=c):
                tin_copy(n, c).wait_send()

        @pl.when(not_last)
        def _(c=c):
            for d in range(SPAN):
                kz_copy(d, c).wait_send()

        @pl.when(not_first)
        def _(c=c):
            dz_copy(c).wait_send()

    for d in around:
        up_copy(d).wait_send()


def hand_over_kernel(dq_in, kv_in, w_in, dq_out, kv_out, w_out):
    dq_out[...] = dq_in[...]
    w_out[...] = w_in[...]
    for n in range(2):
        kv_out[:, n, :] = kv_in[n]


def hand_over(dq, kv, w):
    toks, width = dq.shape
    vm = pl.BlockSpec(memory_space=pltpu.VMEM)
    return pl.pallas_call(
        hand_over_kernel,
        out_shape=(
            jax.ShapeDtypeStruct(dq.shape, dq.dtype),
            jax.ShapeDtypeStruct((toks, 2, width), kv.dtype),
            jax.ShapeDtypeStruct(w.shape, w.dtype),
        ),
        in_specs=[vm] * 3,
        out_specs=(vm,) * 3,
        name="hand_over",
    )(dq, kv, w)


def shards(queries, keys_values, upstream, out_weight):
    seqs, toks, width = queries.shape
    ctx, fsdp = lax.axis_size("ctx"), lax.axis_size("fsdp")
    planes = ctx // SPAN
    model = upstream.shape[2]
    own_rows = model // (ctx * fsdp)
    quarter = width // SPAN
    heads = quarter // HEAD_DIM
    group = SPAN * toks
    dma = pltpu.SemaphoreType.DMA
    any_spec = pl.BlockSpec(memory_space=pl.ANY)
    vm = pl.BlockSpec(memory_space=pltpu.VMEM)
    near = dma((SPAN, heads))
    line = dma((heads,))
    sides = dma((fsdp, heads))
    levels = dma((planes, heads))
    dq, out_kv, out_w = pl.pallas_call(
        functools.partial(layer_kernel, planes, fsdp),
        out_shape=(
            jax.ShapeDtypeStruct((toks, width), BF16),
            jax.ShapeDtypeStruct((2, toks, width), BF16),
            jax.ShapeDtypeStruct((own_rows, width), F32),
        ),
        in_specs=[any_spec] * 4,
        out_specs=(any_spec, any_spec, vm),
        scratch_shapes=[
            pltpu.VMEM((toks, 2, width), BF16),
            pltpu.VMEM((2, toks, width), BF16),
            pltpu.VMEM((group, quarter), BF16),
            pltpu.VMEM((2, 2 * group, quarter), BF16),
            pltpu.VMEM((group, model), BF16),
            pltpu.VMEM((model, group), BF16),
            pltpu.VMEM((model, quarter), BF16),
            pltpu.VMEM((group, quarter), BF16),
            pltpu.VMEM((group, quarter), BF16),
            pltpu.VMEM((heads * SPAN, toks, group + toks), BF16),
            pltpu.VMEM((SPAN, toks, group + toks), F32),
            pltpu.VMEM((group, quarter), BF16),
            pltpu.VMEM((2, 2 * group, quarter), F32),
            pltpu.VMEM((2, group, quarter), BF16),
            pltpu.VMEM((2, group, quarter), BF16),
            pltpu.VMEM((2, group, quarter), BF16),
            pltpu.VMEM((fsdp, model // fsdp, quarter), BF16),
            pltpu.VMEM((fsdp, model // fsdp, quarter), BF16),
            pltpu.VMEM((planes, SPAN * own_rows, quarter), BF16),
            pltpu.VMEM((planes, SPAN * own_rows, quarter), BF16),
            pltpu.VMEM((planes // 2, SPAN * own_rows, quarter), BF16),
            pltpu.VMEM((SPAN, own_rows, quarter), BF16),
            pltpu.VMEM((SPAN, own_rows, quarter), BF16),
            dma((4,)), near, near, near, near, dma((SPAN,)), dma((SPAN,)), sides, sides, near, near,
            near, near, line, line, near, near, sides, sides, levels, levels, levels, dma((planes // 2, heads)), near, near,
        ],
        compiler_params=pltpu.CompilerParams(collective_id=0, has_side_effects=True),
        name="layer",
    )(queries[0], keys_values[0], upstream[0], out_weight)
    dq, out_kv, out_w = hand_over(dq, out_kv, out_w)
    return dq[None], out_kv[None], out_w


def solution(mesh):
    return jax.shard_map(
        shards,
        mesh=mesh,
        in_specs=(
            P("fsdp", "ctx", None),
            P("fsdp", "ctx", None, None),
            P("fsdp", "ctx", None),
            P("fsdp", None),
        ),
        out_specs=(P("fsdp", "ctx", None), P("fsdp", "ctx", None, None), P(("ctx", "fsdp"), None)),
        check_vma=False,
    )
```

```python
import functools

import jax
import jax.numpy as jnp
from jax import lax
from jax.experimental import pallas as pl
from jax.experimental.pallas import tpu as pltpu
from jax.sharding import PartitionSpec as P

HEAD_DIM = 128
SPAN = 4
NEGATIVE = -1e30
F32 = jnp.float32
BF16 = jnp.bfloat16
NT = (((1,), (1,)), ((), ()))
TN = (((0,), (0,)), ((), ()))


def remote(src, dst, send, recv, device):
    return pltpu.make_async_remote_copy(
        src_ref=src, dst_ref=dst, send_sem=send, recv_sem=recv, device_id=device, device_id_type=pl.DeviceIdType.MESH
    )


def layer_kernel(
    planes, fsdp,
    q_in, kv_pairs, up_in, weight,
    dq_out, kv_out, out_w,
    kv_raw, kv_in, q, kv, up, up_t, w, ga, att, low, bias, dq, dkv, dsum, q_next, ga_next, stats, stats_next,
    gw_out, gw_in, zw_out, pin, tin, fin_out, fin_in,
    own_sem, kv_s, kv_r, q_s, q_r, u_s, u_r, w_s, w_r, kz_s, kz_r,
    dq_s, dq_r, dk_s, dk_r, qz_s, qz_r, gz_s, gz_r, st_s, st_r, gx_s, gx_r, pin_s, pin_r, tin_s, tin_r, f_s, f_r,
):
    toks = q_in.shape[0]
    depth = weight.shape[0]
    width = weight.shape[1]
    width_up = up_in.shape[1] // 2
    quarter = width // SPAN
    heads = quarter // HEAD_DIM
    plane_toks = SPAN * toks
    keys = plane_toks + toks
    own_rows = out_w.shape[0]
    plane_rows = SPAN * own_rows
    inv_root = HEAD_DIM ** (-0.5)

    me = lax.axis_index("ctx")
    f = lax.axis_index("fsdp")
    p = lax.div(me, SPAN)
    r = lax.rem(me, SPAN)
    mate = r + 1 - 2 * lax.rem(r, 2)
    peer = [r, mate, lax.rem(r + 2, SPAN), lax.rem(mate + 2, SPAN)]
    not_first = p > 0
    not_last = p < planes - 1

    def dev(p_, r_, f_):
        return {"ctx": p_ * SPAN + r_, "fsdp": f_}

    def near(d):
        return dev(p, peer[d], f)

    def side(df):
        return lax.rem(f + df, fsdp)

    def level(dp):
        return lax.rem(p + dp, planes)

    def rows(i):
        return pl.ds(pl.multiple_of(i * toks, toks), toks)

    def own_plane(i):
        return pl.ds(pl.multiple_of(plane_toks + i * toks, toks), toks)

    def head(c):
        return pl.ds(c * HEAD_DIM, HEAD_DIM)

    def wide_head(i, c):
        return pl.ds(pl.multiple_of(i * quarter + c * HEAD_DIM, HEAD_DIM), HEAD_DIM)

    def quart(i):
        return pl.ds(pl.multiple_of(i * quarter, quarter), quarter)

    def w_rows(i):
        return pl.ds(pl.multiple_of(i * depth, depth), depth)

    pairs_copy = pltpu.make_async_copy(kv_pairs, kv_raw, own_sem.at[0])
    pairs_copy.start()
    own_copies = [
        pltpu.make_async_copy(q_in.at[:, quart(r)], q.at[rows(r), :], own_sem.at[1]),
        pltpu.make_async_copy(up_in, up.at[rows(r), :], own_sem.at[2]),
        pltpu.make_async_copy(weight.at[:, quart(r)], w.at[w_rows(f), :], own_sem.at[3]),
    ]
    for copy in own_copies:
        copy.start()

    sem = pltpu.get_barrier_semaphore()
    targets = [near(d) for d in range(1, SPAN)]
    targets += [dev(p, r, side(df)) for df in range(1, fsdp)]
    targets += [dev(level(dp), r, f) for dp in range(1, planes)]
    for target in targets:
        pl.semaphore_signal(sem, inc=1, device_id=target, device_id_type=pl.DeviceIdType.MESH)
    pairs_copy.wait()
    for n in range(2):
        kv_in[n] = kv_raw[:, n, :]
    pl.semaphore_wait(sem, len(targets))

    def kv_copy(d, c):
        return remote(kv_in.at[:, :, wide_head(peer[d], c)], kv.at[:, own_plane(r), head(c)], kv_s.at[d, c], kv_r.at[d, c], near(d))

    def kv_came(d, c):
        here = kv.at[:, own_plane(peer[d]), head(c)]
        remote(here, here, kv_s.at[d, c], kv_r.at[d, c], near(d)).wait_recv()

    def q_copy(d, c):
        return remote(q_in.at[:, wide_head(peer[d], c)], q.at[rows(r), head(c)], q_s.at[d, c], q_r.at[d, c], near(d))

    def q_came(d, c):
        here = q.at[rows(peer[d]), head(c)]
        remote(here, here, q_s.at[d, c], q_r.at[d, c], near(d)).wait_recv()

    def up_copy(d, h):
        cols = slice(h * width_up, (h + 1) * width_up)
        if d == 3:
            here = up.at[rows(peer[2]), cols]
            return remote(here, here, u_s.at[3, h], u_r.at[3, h], near(1))
        return remote(up_in.at[:, cols], up.at[rows(r), cols], u_s.at[d, h], u_r.at[d, h], near(d))

    def up_came(d, h):
        here = up.at[rows(peer[d]), h * width_up : (h + 1) * width_up]
        remote(here, here, u_s.at[d, h], u_r.at[d, h], near(d)).wait_recv()

    def w_copy(df, c):
        return remote(
            weight.at[:, wide_head(r, c)], w.at[w_rows(f), head(c)], w_s.at[df, c], w_r.at[fsdp - df, c], dev(p, r, side(df))
        )

    def w_came(df, c):
        here = w.at[w_rows(side(df)), head(c)]
        remote(here, here, w_s.at[df, c], w_r.at[df, c], dev(p, r, side(df))).wait_recv()

    def kz_copy(d, c):
        src = kv_in.at[:, :, wide_head(r, c)] if d == 0 else kv.at[:, own_plane(peer[d]), head(c)]
        return remote(src, kv.at[:, rows(peer[d]), head(c)], kz_s.at[d, c], kz_r.at[d, c], dev(p + 1, r, f))

    def block_head(ref, lead, j, c):
        return ref.at[lead + (slice(j * toks, (j + 1) * toks), head(c))]

    def dq_copy(j, c):
        return remote(block_head(dq, (), j, c), dq_out.at[:, wide_head(r, c)], dq_s.at[j, c], dq_r.at[r, c], dev(p, j, f))

    def dq_came(d, c):
        here = dq_out.at[:, wide_head(peer[d], c)]
        remote(here, here, dq_s.at[0, c], dq_r.at[peer[d], c], near(d)).wait_recv()

    def own_dq(j, c):
        return pltpu.make_async_copy(block_head(dq, (), j, c), dq_out.at[:, wide_head(r, c)], dq_s.at[j, c])

    def qz_copy(d, c):
        src = q_in.at[:, wide_head(r, c)] if d == 0 else q.at[rows(peer[d]), head(c)]
        return remote(src, q_next.at[rows(peer[d]), head(c)], qz_s.at[d, c], qz_r.at[d, c], dev(p - 1, r, f))

    def ga_copy(c):
        return remote(ga.at[:, head(c)], ga_next.at[:, head(c)], gz_s.at[c], gz_r.at[c], dev(p - 1, r, f))

    def stats_copy(c):
        return remote(stats.at[c], stats_next.at[c], st_s.at[c], st_r.at[c], dev(p - 1, r, f))

    def dk_copy(j, c):
        return remote(block_head(dsum, (slice(None),), j, c), kv_out.at[:, :, wide_head(r, c)], dk_s.at[j, c], dk_r.at[r, c], dev(p, j, f))

    def dk_came(d, c):
        here = kv_out.at[:, :, wide_head(peer[d], c)]
        remote(here, here, dk_s.at[0, c], dk_r.at[peer[d], c], near(d)).wait_recv()

    def own_dk(j, c):
        return pltpu.make_async_copy(block_head(dsum, (slice(None),), j, c), kv_out.at[:, :, wide_head(r, c)], dk_s.at[j, c])

    def hand(j, own, other):
        @pl.when(r == j)
        def _():
            own()

        @pl.when(r != j)
        def _():
            other()

    def gx_copy(df, c):
        return remote(
            gw_out.at[side(df), :, head(c)], gw_in.at[fsdp - df, :, head(c)], gx_s.at[df, c], gx_r.at[fsdp - df, c],
            dev(p, r, side(df)),
        )

    def gx_came(df, c):
        here = gw_in.at[df, :, head(c)]
        remote(here, here, gx_s.at[df, c], gx_r.at[df, c], dev(p, r, side(df))).wait_recv()

    lower = lax.rem(p, 2) == 0
    partner = dev(p + 1 - 2 * lax.rem(p, 2), r, f)
    group = lax.div(p, 2)

    def to_partner(n):
        return jnp.logical_or(jnp.logical_and(lower, n > p), jnp.logical_and(jnp.logical_not(lower), n < p))

    def to_plane(n):
        return jnp.logical_or(jnp.logical_and(lower, n < p), jnp.logical_and(jnp.logical_not(lower), n > p))

    def pin_copy(n, c):
        return remote(zw_out.at[n, :, head(c)], pin.at[n, :, head(c)], pin_s.at[n, c], pin_r.at[n, c], partner)

    def tin_copy(n, c):
        return remote(zw_out.at[n, :, head(c)], tin.at[group, :, head(c)], tin_s.at[n, c], tin_r.at[group, c], dev(n, r, f))

    def tin_came(k, c):
        here = tin.at[k, :, head(c)]
        remote(here, here, tin_s.at[0, c], tin_r.at[k, c], partner).wait_recv()

    def f_copy(d, c):
        return remote(fin_out.at[peer[d], :, head(c)], fin_in.at[r, :, head(c)], f_s.at[d, c], f_r.at[d, c], near(d))

    def f_came(d, c):
        here = fin_in.at[peer[d], :, head(c)]
        remote(here, here, f_s.at[d, c], f_r.at[d, c], near(d)).wait_recv()

    around = range(1, SPAN)

    def spread(c):
        for d in around:
            kv_copy(d, c).start()
        for d in around:
            q_copy(d, c).start()

        @pl.when(not_first)
        def _():
            qz_copy(0, c).start()

    def halo(c):
        @pl.when(not_last)
        def _():
            kz_copy(0, c).start()

    def columns(c):
        for df in range(1, fsdp):
            w_copy(df, c).start()

    def lift():
        for h in range(2):
            up_copy(2, h).start()
        for h in range(2):
            up_copy(1, h).start()

    columns(1)
    halo(2)
    spread(2)
    halo(0)
    lift()
    spread(0)
    columns(3)
    columns(2)
    spread(3)
    halo(3)
    columns(0)
    halo(1)
    spread(1)
    row = lax.broadcasted_iota(jnp.int32, (toks, keys), 0)
    col = lax.broadcasted_iota(jnp.int32, (toks, keys), 1)
    for b in range(SPAN):
        first = jnp.where(not_first, 0, plane_toks - b * toks)
        bias[b] = jnp.where((col > row) & (col <= row + plane_toks) & (col >= first), 0.0, NEGATIVE)
    dkv[...] = jnp.zeros(dkv.shape, F32)
    stats[...] = jnp.zeros(stats.shape, F32)

    @pl.when(p == 0)
    def _():
        kv[:, :plane_toks] = jnp.zeros((2, plane_toks, quarter), BF16)

    def forward(c):
        for d in around:
            kv_came(d, c)

            @pl.when(not_last)
            def _(d=d):
                kz_copy(d, c).start()

    def forward_q(c):
        for d in around:
            q_came(d, c)

            @pl.when(not_first)
            def _(d=d):
                qz_copy(d, c).start()

    diagonal = lax.broadcasted_iota(jnp.int32, (toks, toks), 0) == lax.broadcasted_iota(jnp.int32, (toks, toks), 1)

    def as_row(column):
        return jnp.sum(jnp.where(diagonal, column, 0.0), axis=0, keepdims=True)

    def window(b):
        return pl.ds(b * toks, keys)

    def attend(c):
        @pl.when(not_first)
        def _():
            for d in range(SPAN):
                here = kv.at[:, rows(peer[d]), head(c)]
                remote(here, here, kz_s.at[d, c], kz_r.at[d, c], near(1)).wait_recv()

        for b in range(SPAN):
            block = pl.ds(b * toks, toks)
            scores = lax.dot_general(q[block, head(c)], kv[0, window(b), head(c)], NT, preferred_element_type=F32) * inv_root + bias[b]
            top = jnp.max(scores, axis=-1, keepdims=True)
            lifted = jnp.exp(scores - top)
            mass = jnp.sum(lifted, axis=-1, keepdims=True)
            stats[c, 0:1, block] = as_row(top + jnp.log(mass))
            prob = (lifted * (1.0 / mass)).astype(BF16)
            low[c * SPAN + b] = prob
            att[block, head(c)] = jnp.dot(prob, kv[1, window(b), head(c)], preferred_element_type=F32).astype(BF16)

    def center_of(block, c):
        return jnp.sum(ga[block, head(c)].astype(F32) * att[block, head(c)].astype(F32), axis=-1, keepdims=True)

    def send_down(c):
        @pl.when(not_first)
        def _():
            for b in range(SPAN):
                block = pl.ds(b * toks, toks)
                stats[c, 1:2, block] = as_row(center_of(block, c))
            ga_copy(c).start()
            stats_copy(c).start()

    def backward(c):
        for b in range(SPAN):
            block = pl.ds(b * toks, toks)
            g = ga[block, head(c)]
            prob = low[c * SPAN + b]
            k = kv[0, window(b), head(c)]
            products = lax.dot_general(g, kv[1, window(b), head(c)], NT, preferred_element_type=F32)
            ds = (prob.astype(F32) * (products - center_of(block, c))).astype(BF16)
            dq[block, head(c)] = (jnp.dot(ds, k, preferred_element_type=F32) * inv_root).astype(BF16)
            seen = slice(plane_toks - b * toks, keys)
            mine = slice(0, (b + 1) * toks)
            dkv[0, mine, head(c)] += lax.dot_general(ds[:, seen], q[block, head(c)], TN, preferred_element_type=F32) * inv_root
            dkv[1, mine, head(c)] += lax.dot_general(prob[:, seen], g, TN, preferred_element_type=F32)
        for j in range(SPAN):
            hand(j, lambda: own_dq(j, c).start(), lambda: dq_copy(j, c).start())

    def next_plane(c):
        @pl.when(not_last)
        def _():
            for d in range(SPAN):
                here = q_next.at[rows(peer[d]), head(c)]
                remote(here, here, qz_s.at[d, c], qz_r.at[d, c], near(1)).wait_recv()
            ga_copy(c).wait_recv()
            stats_copy(c).wait_recv()
            for b in range(SPAN):
                block = pl.ds(b * toks, toks)
                count = plane_toks - b * toks
                mine = slice(b * toks, plane_toks)
                seen = slice(plane_toks + b * toks, 2 * plane_toks)
                shape = (count, toks)
                visible = lax.broadcasted_iota(jnp.int32, shape, 0) > lax.broadcasted_iota(jnp.int32, shape, 1)
                qn, gn = q_next[block, head(c)], ga_next[block, head(c)]
                scores = lax.dot_general(kv[0, seen, head(c)], qn, NT, preferred_element_type=F32) * inv_root
                prob = jnp.exp(jnp.where(visible, scores - stats_next[c, 0:1, block], NEGATIVE))
                products = lax.dot_general(kv[1, seen, head(c)], gn, NT, preferred_element_type=F32)
                ds = (prob * (products - stats_next[c, 1:2, block])).astype(BF16)
                dkv[0, mine, head(c)] += jnp.dot(ds, qn, preferred_element_type=F32) * inv_root
                dkv[1, mine, head(c)] += jnp.dot(prob.astype(BF16), gn, preferred_element_type=F32)

    def return_kv(c):
        dsum[:, :, head(c)] = dkv[:, :, head(c)].astype(BF16)
        for j in range(SPAN):
            hand(j, lambda: own_dk(j, c).start(), lambda: dk_copy(j, c).start())

    def project(c, d):
        if d == 0:
            for df in range(1, fsdp):
                w_came(df, c)
        ga[rows(peer[d]), head(c)] = jnp.dot(up[rows(peer[d]), :], w[:, head(c)], preferred_element_type=F32).astype(BF16)

    def turn(d):
        up_t[:, rows(peer[d])] = up[rows(peer[d]), :].T

    tile = plane_toks
    unit = fsdp * own_rows

    def weigh(c):
        def step(t, _):
            value = jnp.dot(up_t[pl.ds(pl.multiple_of(t * tile, tile), tile), :], att[:, head(c)], preferred_element_type=F32)
            value = value.reshape(tile // unit, fsdp, own_rows, HEAD_DIM)
            part = tile // fsdp
            for n in range(fsdp):
                gw_out[n, pl.ds(pl.multiple_of(t * part, part), part), head(c)] = value[:, n].reshape(part, HEAD_DIM).astype(BF16)
            return 0

        lax.fori_loop(0, up_t.shape[0] // tile, step, 0)
        for df in range(1, fsdp):
            gx_copy(df, c).start()

    def merge(c):
        total = gw_out[f, :, head(c)].astype(F32)
        for df in range(1, fsdp):
            gx_came(df, c)
            total = total + gw_in[df, :, head(c)].astype(F32)
        for n in range(planes):
            zw_out[n, :, head(c)] = total[n * plane_rows : (n + 1) * plane_rows].astype(BF16)
        for n in range(planes):
            @pl.when(to_partner(n))
            def _(n=n):
                pin_copy(n, c).start()

    def relay(c):
        for n in range(planes):
            @pl.when(to_plane(n))
            def _(n=n):
                pin_copy(n, c).wait_recv()
                zw_out[n, :, head(c)] = (zw_out[n, :, head(c)].astype(F32) + pin[n, :, head(c)].astype(F32)).astype(BF16)
                tin_copy(n, c).start()

    def total_up(c):
        pin_copy(p, c).wait_recv()
        total = zw_out[p, :, head(c)].astype(F32) + pin[p, :, head(c)].astype(F32)
        for dk in range(1, planes // 2):
            k = lax.rem(group + dk, planes // 2)
            tin_came(k, c)
            total = total + tin[k, :, head(c)].astype(F32)
        for n in range(SPAN):
            fin_out[n, :, head(c)] = total[n * own_rows : (n + 1) * own_rows].astype(BF16)
        for d in (2, 3, 1):
            f_copy(d, c).start()

    def finish(c):
        for d in around:
            f_came(d, c)
        out_w[:, wide_head(r, c)] = fin_out[r, :, head(c)].astype(F32)
        for d in around:
            out_w[:, wide_head(peer[d], c)] = fin_in[peer[d], :, head(c)].astype(F32)

    def settle():
        kv[:, own_plane(r), :] = kv_in[:, :, quart(r)]
        for copy in own_copies:
            copy.wait()
        for h in range(2):
            up_came(1, h)
        turn(0)
        turn(1)

    def lift_on(h):
        up_came(2, h)
        up_copy(3, h).start()

    def lift_end():
        turn(2)
        for h in range(2):
            up_came(3, h)
        turn(3)

    def project_chip(c):
        project(c, 0)
        project(c, 1)

    def project_rest(c):
        project(c, 2)
        project(c, 3)

    settle()
    lift_on(0)
    forward(2)
    lift_on(1)
    forward_q(2)
    attend(2)
    project_chip(2)
    lift_end()
    project_rest(2)
    forward(0)
    send_down(2)
    weigh(2)
    forward_q(0)
    forward(3)
    project_chip(0)
    project_rest(0)
    forward_q(3)
    attend(0)
    send_down(0)
    project_chip(1)
    project_chip(3)
    project_rest(3)
    forward(1)
    weigh(0)
    forward_q(1)
    attend(3)
    merge(2)
    weigh(3)
    send_down(3)
    attend(1)
    next_plane(2)
    project_rest(1)
    merge(0)
    backward(2)
    send_down(1)
    return_kv(2)
    backward(0)
    weigh(1)
    next_plane(0)
    return_kv(0)
    relay(2)
    backward(3)
    merge(3)
    relay(0)
    next_plane(3)
    return_kv(3)
    next_plane(1)
    merge(1)
    relay(3)
    total_up(0)
    backward(1)
    finish(0)
    return_kv(1)
    total_up(2)
    relay(1)
    total_up(3)
    total_up(1)
    finish(3)
    finish(2)
    finish(1)
    for c in range(heads):
        for d in around:
            dq_came(d, c)
            dk_came(d, c)
            for copy in (kv_copy(d, c), q_copy(d, c), f_copy(d, c)):
                copy.wait_send()
        for j in range(SPAN):
            hand(j, lambda: own_dq(j, c).wait(), lambda: dq_copy(j, c).wait_send())
            hand(j, lambda: own_dk(j, c).wait(), lambda: dk_copy(j, c).wait_send())
        for df in range(1, fsdp):
            w_copy(df, c).wait_send()
            gx_copy(df, c).wait_send()
        for n in range(planes):
            @pl.when(to_partner(n))
            def _(n=n, c=c):
                pin_copy(n, c).wait_send()

            @pl.when(to_plane(n))
            def _(n=n, c=c):
                tin_copy(n, c).wait_send()

        @pl.when(not_last)
        def _(c=c):
            for d in range(SPAN):
                kz_copy(d, c).wait_send()

        @pl.when(not_first)
        def _(c=c):
            for d in range(SPAN):
                qz_copy(d, c).wait_send()
            ga_copy(c).wait_send()
            stats_copy(c).wait_send()

    for d in around:
        for h in range(2):
            up_copy(d, h).wait_send()


def hand_over_kernel(dq_in, kv_in, w_in, dq_out, kv_out, w_out):
    dq_out[...] = dq_in[...]
    w_out[...] = w_in[...]
    for n in range(2):
        kv_out[:, n, :] = kv_in[n]


def hand_over(dq, kv, w):
    toks, width = dq.shape
    vm = pl.BlockSpec(memory_space=pltpu.VMEM)
    return pl.pallas_call(
        hand_over_kernel,
        out_shape=(
            jax.ShapeDtypeStruct(dq.shape, dq.dtype),
            jax.ShapeDtypeStruct((toks, 2, width), kv.dtype),
            jax.ShapeDtypeStruct(w.shape, w.dtype),
        ),
        in_specs=[vm] * 3,
        out_specs=(vm,) * 3,
        name="hand_over",
    )(dq, kv, w)


def shards(queries, keys_values, upstream, out_weight):
    seqs, toks, width = queries.shape
    ctx, fsdp = lax.axis_size("ctx"), lax.axis_size("fsdp")
    planes = ctx // SPAN
    model = upstream.shape[2]
    own_rows = model // (ctx * fsdp)
    quarter = width // SPAN
    heads = quarter // HEAD_DIM
    group = SPAN * toks
    dma = pltpu.SemaphoreType.DMA
    any_spec = pl.BlockSpec(memory_space=pl.ANY)
    vm = pl.BlockSpec(memory_space=pltpu.VMEM)
    near = dma((SPAN, heads))
    sides = dma((fsdp, heads))
    levels = dma((planes, heads))
    dq, out_kv, out_w = pl.pallas_call(
        functools.partial(layer_kernel, planes, fsdp),
        out_shape=(
            jax.ShapeDtypeStruct((toks, width), BF16),
            jax.ShapeDtypeStruct((2, toks, width), BF16),
            jax.ShapeDtypeStruct((own_rows, width), F32),
        ),
        in_specs=[any_spec] * 4,
        out_specs=(any_spec, any_spec, vm),
        scratch_shapes=[
            pltpu.VMEM((toks, 2, width), BF16),
            pltpu.VMEM((2, toks, width), BF16),
            pltpu.VMEM((group, quarter), BF16),
            pltpu.VMEM((2, 2 * group, quarter), BF16),
            pltpu.VMEM((group, model), BF16),
            pltpu.VMEM((model, group), BF16),
            pltpu.VMEM((model, quarter), BF16),
            pltpu.VMEM((group, quarter), BF16),
            pltpu.VMEM((group, quarter), BF16),
            pltpu.VMEM((heads * SPAN, toks, group + toks), BF16),
            pltpu.VMEM((SPAN, toks, group + toks), F32),
            pltpu.VMEM((group, quarter), BF16),
            pltpu.VMEM((2, group, quarter), F32),
            pltpu.VMEM((2, group, quarter), BF16),
            pltpu.VMEM((group, quarter), BF16),
            pltpu.VMEM((group, quarter), BF16),
            pltpu.VMEM((heads, 8, group), F32),
            pltpu.VMEM((heads, 8, group), F32),
            pltpu.VMEM((fsdp, model // fsdp, quarter), BF16),
            pltpu.VMEM((fsdp, model // fsdp, quarter), BF16),
            pltpu.VMEM((planes, SPAN * own_rows, quarter), BF16),
            pltpu.VMEM((planes, SPAN * own_rows, quarter), BF16),
            pltpu.VMEM((planes // 2, SPAN * own_rows, quarter), BF16),
            pltpu.VMEM((SPAN, own_rows, quarter), BF16),
            pltpu.VMEM((SPAN, own_rows, quarter), BF16),
            dma((4,)), near, near, near, near, dma((SPAN, 2)), dma((SPAN, 2)), sides, sides, near, near,
            near, near, near, near, near, near, dma((heads,)), dma((heads,)), dma((heads,)), dma((heads,)), sides, sides, levels, levels, levels, dma((planes // 2, heads)), near, near,
        ],
        compiler_params=pltpu.CompilerParams(collective_id=0, has_side_effects=True),
        name="layer",
    )(queries[0], keys_values[0], upstream[0], out_weight)
    dq, out_kv, out_w = hand_over(dq, out_kv, out_w)
    return dq[None], out_kv[None], out_w


def solution(mesh):
    return jax.shard_map(
        shards,
        mesh=mesh,
        in_specs=(
            P("fsdp", "ctx", None),
            P("fsdp", "ctx", None, None),
            P("fsdp", "ctx", None),
            P("fsdp", None),
        ),
        out_specs=(P("fsdp", "ctx", None), P("fsdp", "ctx", None, None), P(("ctx", "fsdp"), None)),
        check_vma=False,
    )
```

```python
import functools

import jax
import jax.numpy as jnp
from jax import lax
from jax.experimental import pallas as pl
from jax.experimental.pallas import tpu as pltpu
from jax.sharding import PartitionSpec as P

HEAD_DIM = 128
SPAN = 4
NEGATIVE = -1e30
F32 = jnp.float32
BF16 = jnp.bfloat16
NT = (((1,), (1,)), ((), ()))
TN = (((0,), (0,)), ((), ()))


def remote(src, dst, send, recv, device):
    return pltpu.make_async_remote_copy(
        src_ref=src, dst_ref=dst, send_sem=send, recv_sem=recv, device_id=device, device_id_type=pl.DeviceIdType.MESH
    )


def layer_kernel(
    planes, fsdp,
    q_in, kv_pairs, up_in, weight,
    dq_out, kv_out, out_w,
    kv_raw, kv_in, q, kv, up, up_t, w, ga, att, low, bias, dq, dkv, dsum, q_next, ga_next, stats, stats_next,
    gw_out, gw_in, zw_out, pin, tin, fin_out, fin_in,
    own_sem, kv_s, kv_r, q_s, q_r, u_s, u_r, w_s, w_r, wz_s, wz_r, kz_s, kz_r,
    dq_s, dq_r, dk_s, dk_r, qz_s, qz_r, gz_s, gz_r, st_s, st_r, gx_s, gx_r, pin_s, pin_r, tin_s, tin_r, f_s, f_r,
):
    toks = q_in.shape[0]
    depth = weight.shape[0]
    width = weight.shape[1]
    width_up = up_in.shape[1] // 2
    quarter = width // SPAN
    heads = quarter // HEAD_DIM
    plane_toks = SPAN * toks
    keys = plane_toks + toks
    own_rows = out_w.shape[0]
    plane_rows = SPAN * own_rows
    inv_root = HEAD_DIM ** (-0.5)

    me = lax.axis_index("ctx")
    f = lax.axis_index("fsdp")
    p = lax.div(me, SPAN)
    r = lax.rem(me, SPAN)
    mate = r + 1 - 2 * lax.rem(r, 2)
    peer = [r, mate, lax.rem(r + 2, SPAN), lax.rem(mate + 2, SPAN)]
    not_first = p > 0
    not_last = p < planes - 1

    def dev(p_, r_, f_):
        return {"ctx": p_ * SPAN + r_, "fsdp": f_}

    def near(d):
        return dev(p, peer[d], f)

    def side(df):
        return lax.rem(f + df, fsdp)

    def level(dp):
        return lax.rem(p + dp, planes)

    def rows(i):
        return pl.ds(pl.multiple_of(i * toks, toks), toks)

    def own_plane(i):
        return pl.ds(pl.multiple_of(plane_toks + i * toks, toks), toks)

    def head(c):
        return pl.ds(c * HEAD_DIM, HEAD_DIM)

    def wide_head(i, c):
        return pl.ds(pl.multiple_of(i * quarter + c * HEAD_DIM, HEAD_DIM), HEAD_DIM)

    def quart(i):
        return pl.ds(pl.multiple_of(i * quarter, quarter), quarter)

    def w_rows(i):
        return pl.ds(pl.multiple_of(i * depth, depth), depth)

    pairs_copy = pltpu.make_async_copy(kv_pairs, kv_raw, own_sem.at[0])
    pairs_copy.start()
    own_copies = [
        pltpu.make_async_copy(q_in.at[:, quart(r)], q.at[rows(r), :], own_sem.at[1]),
        pltpu.make_async_copy(up_in, up.at[rows(r), :], own_sem.at[2]),
        pltpu.make_async_copy(weight.at[:, quart(r)], w.at[w_rows(f), :], own_sem.at[3]),
    ]
    for copy in own_copies:
        copy.start()

    sem = pltpu.get_barrier_semaphore()
    targets = [near(d) for d in range(1, SPAN)]
    targets += [dev(p, r, side(df)) for df in range(1, fsdp)]
    targets += [dev(level(dp), r, f) for dp in range(1, planes)]
    for target in targets:
        pl.semaphore_signal(sem, inc=1, device_id=target, device_id_type=pl.DeviceIdType.MESH)
    pairs_copy.wait()
    for n in range(2):
        kv_in[n] = kv_raw[:, n, :]
    pl.semaphore_wait(sem, len(targets))

    def kv_copy(d, c):
        return remote(kv_in.at[:, :, wide_head(peer[d], c)], kv.at[:, own_plane(r), head(c)], kv_s.at[d, c], kv_r.at[d, c], near(d))

    def kv_came(d, c):
        here = kv.at[:, own_plane(peer[d]), head(c)]
        remote(here, here, kv_s.at[d, c], kv_r.at[d, c], near(d)).wait_recv()

    def q_copy(d, c):
        return remote(q_in.at[:, wide_head(peer[d], c)], q.at[rows(r), head(c)], q_s.at[d, c], q_r.at[d, c], near(d))

    def q_came(d, c):
        here = q.at[rows(peer[d]), head(c)]
        remote(here, here, q_s.at[d, c], q_r.at[d, c], near(d)).wait_recv()

    def up_copy(d, h):
        cols = slice(h * width_up, (h + 1) * width_up)
        if d == 3:
            here = up.at[rows(peer[2]), cols]
            return remote(here, here, u_s.at[3, h], u_r.at[3, h], near(1))
        return remote(up_in.at[:, cols], up.at[rows(r), cols], u_s.at[d, h], u_r.at[d, h], near(d))

    def up_came(d, h):
        here = up.at[rows(peer[d]), h * width_up : (h + 1) * width_up]
        remote(here, here, u_s.at[d, h], u_r.at[d, h], near(d)).wait_recv()

    def w_copy(df, c):
        return remote(
            weight.at[:, wide_head(r, c)], w.at[w_rows(f), head(c)], w_s.at[df, c], w_r.at[fsdp - df, c], dev(p, r, side(df))
        )

    def w_came(df, c):
        here = w.at[w_rows(side(df)), head(c)]
        remote(here, here, w_s.at[df, c], w_r.at[df, c], dev(p, r, side(df))).wait_recv()

    lower = lax.rem(p, 2) == 0
    upper = jnp.logical_not(lower)
    partner = dev(p + 1 - 2 * lax.rem(p, 2), r, f)

    def wz_copy(df, c):
        here = w.at[w_rows(side(df)), head(c)]
        return remote(here, here, wz_s.at[df, c], wz_r.at[df, c], partner)

    def by_side(c):
        if c == heads - 2:
            return lower
        if c == heads - 1:
            return upper
        return None

    def kz_copy(d, c):
        src = kv_in.at[:, :, wide_head(r, c)] if d == 0 else kv.at[:, own_plane(peer[d]), head(c)]
        return remote(src, kv.at[:, rows(peer[d]), head(c)], kz_s.at[d, c], kz_r.at[d, c], dev(p + 1, r, f))

    def block_head(ref, lead, j, c):
        return ref.at[lead + (slice(j * toks, (j + 1) * toks), head(c))]

    def dq_copy(j, c):
        return remote(block_head(dq, (), j, c), dq_out.at[:, wide_head(r, c)], dq_s.at[j, c], dq_r.at[r, c], dev(p, j, f))

    def dq_came(d, c):
        here = dq_out.at[:, wide_head(peer[d], c)]
        remote(here, here, dq_s.at[0, c], dq_r.at[peer[d], c], near(d)).wait_recv()

    def own_dq(j, c):
        return pltpu.make_async_copy(block_head(dq, (), j, c), dq_out.at[:, wide_head(r, c)], dq_s.at[j, c])

    def qz_copy(d, c):
        src = q_in.at[:, wide_head(r, c)] if d == 0 else q.at[rows(peer[d]), head(c)]
        return remote(src, q_next.at[rows(peer[d]), head(c)], qz_s.at[d, c], qz_r.at[d, c], dev(p - 1, r, f))

    def ga_copy(c):
        return remote(ga.at[:, head(c)], ga_next.at[:, head(c)], gz_s.at[c], gz_r.at[c], dev(p - 1, r, f))

    def stats_copy(c):
        return remote(stats.at[c], stats_next.at[c], st_s.at[c], st_r.at[c], dev(p - 1, r, f))

    def dk_copy(j, c):
        return remote(block_head(dsum, (slice(None),), j, c), kv_out.at[:, :, wide_head(r, c)], dk_s.at[j, c], dk_r.at[r, c], dev(p, j, f))

    def dk_came(d, c):
        here = kv_out.at[:, :, wide_head(peer[d], c)]
        remote(here, here, dk_s.at[0, c], dk_r.at[peer[d], c], near(d)).wait_recv()

    def own_dk(j, c):
        return pltpu.make_async_copy(block_head(dsum, (slice(None),), j, c), kv_out.at[:, :, wide_head(r, c)], dk_s.at[j, c])

    def hand(j, own, other):
        @pl.when(r == j)
        def _():
            own()

        @pl.when(r != j)
        def _():
            other()

    def gx_copy(df, n, c):
        return remote(
            gw_out.at[side(df), n, :, head(c)], gw_in.at[fsdp - df, n, :, head(c)], gx_s.at[df, n, c], gx_r.at[fsdp - df, n, c],
            dev(p, r, side(df)),
        )

    def gx_came(df, n, c):
        here = gw_in.at[df, n, :, head(c)]
        remote(here, here, gx_s.at[df, n, c], gx_r.at[df, n, c], dev(p, r, side(df))).wait_recv()

    group = lax.div(p, 2)
    far_first = [lax.rem(2 * (group + 1) + i, planes) for i in range(planes - 2)] + [p + 1 - 2 * lax.rem(p, 2), p]

    def to_partner(n):
        return jnp.logical_or(jnp.logical_and(lower, n > p), jnp.logical_and(upper, n < p))

    def to_plane(n):
        return jnp.logical_or(jnp.logical_and(lower, n < p), jnp.logical_and(upper, n > p))

    def pin_copy(n, c):
        return remote(zw_out.at[n, :, head(c)], pin.at[n, :, head(c)], pin_s.at[n, c], pin_r.at[n, c], partner)

    def tin_copy(n, c):
        return remote(zw_out.at[n, :, head(c)], tin.at[group, :, head(c)], tin_s.at[n, c], tin_r.at[group, c], dev(n, r, f))

    def tin_came(k, c):
        here = tin.at[k, :, head(c)]
        remote(here, here, tin_s.at[0, c], tin_r.at[k, c], partner).wait_recv()

    def f_copy(d, c):
        return remote(fin_out.at[peer[d], :, head(c)], fin_in.at[r, :, head(c)], f_s.at[d, c], f_r.at[d, c], near(d))

    def f_came(d, c):
        here = fin_in.at[peer[d], :, head(c)]
        remote(here, here, f_s.at[d, c], f_r.at[d, c], near(d)).wait_recv()

    around = range(1, SPAN)

    def spread(c):
        for d in around:
            kv_copy(d, c).start()
        for d in around:
            q_copy(d, c).start()

        @pl.when(not_first)
        def _():
            qz_copy(0, c).start()

    def halo(c):
        @pl.when(not_last)
        def _():
            kz_copy(0, c).start()

    def columns(c):
        def go():
            for df in range(1, fsdp):
                w_copy(df, c).start()

        if by_side(c) is None:
            go()
        else:
            pl.when(by_side(c))(go)

    def pass_columns():
        for c in (heads - 2, heads - 1):
            @pl.when(by_side(c))
            def _(c=c):
                for df in range(1, fsdp):
                    w_came(df, c)
                    wz_copy(df, c).start()

    def lift():
        for h in range(2):
            up_copy(2, h).start()
        for h in range(2):
            up_copy(1, h).start()

    columns(2)
    spread(0)
    lift()
    halo(0)
    halo(1)
    columns(0)
    columns(3)
    columns(1)
    halo(3)
    spread(1)
    spread(2)
    spread(3)
    halo(2)
    row = lax.broadcasted_iota(jnp.int32, (toks, keys), 0)
    col = lax.broadcasted_iota(jnp.int32, (toks, keys), 1)
    for b in range(SPAN):
        first = jnp.where(not_first, 0, plane_toks - b * toks)
        bias[b] = jnp.where((col > row) & (col <= row + plane_toks) & (col >= first), 0.0, NEGATIVE)
    dkv[...] = jnp.zeros(dkv.shape, F32)
    stats[...] = jnp.zeros(stats.shape, F32)

    @pl.when(p == 0)
    def _():
        kv[:, :plane_toks] = jnp.zeros((2, plane_toks, quarter), BF16)

    def forward(c):
        for d in around:
            kv_came(d, c)

            @pl.when(not_last)
            def _(d=d):
                kz_copy(d, c).start()

    def forward_q(c):
        for d in around:
            q_came(d, c)

            @pl.when(not_first)
            def _(d=d):
                qz_copy(d, c).start()

    diagonal = lax.broadcasted_iota(jnp.int32, (toks, toks), 0) == lax.broadcasted_iota(jnp.int32, (toks, toks), 1)

    def as_row(column):
        return jnp.sum(jnp.where(diagonal, column, 0.0), axis=0, keepdims=True)

    def window(b):
        return pl.ds(b * toks, keys)

    def attend(c):
        @pl.when(not_first)
        def _():
            for d in range(SPAN):
                here = kv.at[:, rows(peer[d]), head(c)]
                remote(here, here, kz_s.at[d, c], kz_r.at[d, c], near(1)).wait_recv()

        for b in range(SPAN):
            block = pl.ds(b * toks, toks)
            scores = lax.dot_general(q[block, head(c)], kv[0, window(b), head(c)], NT, preferred_element_type=F32) * inv_root + bias[b]
            top = jnp.max(scores, axis=-1, keepdims=True)
            lifted = jnp.exp(scores - top)
            mass = jnp.sum(lifted, axis=-1, keepdims=True)
            stats[c, 0:1, block] = as_row(top + jnp.log(mass))
            prob = (lifted * (1.0 / mass)).astype(BF16)
            low[c * SPAN + b] = prob
            att[block, head(c)] = jnp.dot(prob, kv[1, window(b), head(c)], preferred_element_type=F32).astype(BF16)

    def center_of(block, c):
        return jnp.sum(ga[block, head(c)].astype(F32) * att[block, head(c)].astype(F32), axis=-1, keepdims=True)

    def send_down(c):
        @pl.when(not_first)
        def _():
            for b in range(SPAN):
                block = pl.ds(b * toks, toks)
                stats[c, 1:2, block] = as_row(center_of(block, c))
            ga_copy(c).start()
            stats_copy(c).start()

    def backward(c):
        for b in range(SPAN):
            block = pl.ds(b * toks, toks)
            g = ga[block, head(c)]
            prob = low[c * SPAN + b]
            k = kv[0, window(b), head(c)]
            products = lax.dot_general(g, kv[1, window(b), head(c)], NT, preferred_element_type=F32)
            ds = (prob.astype(F32) * (products - center_of(block, c))).astype(BF16)
            dq[block, head(c)] = (jnp.dot(ds, k, preferred_element_type=F32) * inv_root).astype(BF16)
            seen = slice(plane_toks - b * toks, keys)
            mine = slice(0, (b + 1) * toks)
            dkv[0, mine, head(c)] += lax.dot_general(ds[:, seen], q[block, head(c)], TN, preferred_element_type=F32) * inv_root
            dkv[1, mine, head(c)] += lax.dot_general(prob[:, seen], g, TN, preferred_element_type=F32)
        for j in range(SPAN):
            hand(j, lambda: own_dq(j, c).start(), lambda: dq_copy(j, c).start())

    def next_plane(c):
        @pl.when(not_last)
        def _():
            for d in range(SPAN):
                here = q_next.at[rows(peer[d]), head(c)]
                remote(here, here, qz_s.at[d, c], qz_r.at[d, c], near(1)).wait_recv()
            ga_copy(c).wait_recv()
            stats_copy(c).wait_recv()
            for b in range(SPAN):
                block = pl.ds(b * toks, toks)
                count = plane_toks - b * toks
                mine = slice(b * toks, plane_toks)
                seen = slice(plane_toks + b * toks, 2 * plane_toks)
                shape = (count, toks)
                visible = lax.broadcasted_iota(jnp.int32, shape, 0) > lax.broadcasted_iota(jnp.int32, shape, 1)
                qn, gn = q_next[block, head(c)], ga_next[block, head(c)]
                scores = lax.dot_general(kv[0, seen, head(c)], qn, NT, preferred_element_type=F32) * inv_root
                prob = jnp.exp(jnp.where(visible, scores - stats_next[c, 0:1, block], NEGATIVE))
                products = lax.dot_general(kv[1, seen, head(c)], gn, NT, preferred_element_type=F32)
                ds = (prob * (products - stats_next[c, 1:2, block])).astype(BF16)
                dkv[0, mine, head(c)] += jnp.dot(ds, qn, preferred_element_type=F32) * inv_root
                dkv[1, mine, head(c)] += jnp.dot(prob.astype(BF16), gn, preferred_element_type=F32)

    def return_kv(c):
        dsum[:, :, head(c)] = dkv[:, :, head(c)].astype(BF16)
        for j in range(SPAN):
            hand(j, lambda: own_dk(j, c).start(), lambda: dk_copy(j, c).start())

    def project(c, d):
        if d == 0:
            for df in range(1, fsdp):
                if by_side(c) is None:
                    w_came(df, c)
                else:
                    pl.when(jnp.logical_not(by_side(c)))(lambda df=df: wz_copy(df, c).wait_recv())
        ga[rows(peer[d]), head(c)] = jnp.dot(up[rows(peer[d]), :], w[:, head(c)], preferred_element_type=F32).astype(BF16)

    def turn(d):
        up_t[:, rows(peer[d])] = up[rows(peer[d]), :].T

    tile = up_in.shape[1] // planes

    def weigh(c):
        for n in far_first:
            rows_n = pl.ds(pl.multiple_of(n * tile, tile), tile)
            value = jnp.dot(up_t[rows_n, :], att[:, head(c)], preferred_element_type=F32)
            value = value.reshape(SPAN, fsdp, own_rows, HEAD_DIM)
            for i in range(fsdp):
                gw_out[i, n, :, head(c)] = value[:, i].reshape(plane_rows, HEAD_DIM).astype(BF16)
            for df in range(1, fsdp):
                gx_copy(df, n, c).start()

    def merge(c):
        for n in far_first:
            total = gw_out[f, n, :, head(c)].astype(F32)
            for df in range(1, fsdp):
                gx_came(df, n, c)
                total = total + gw_in[df, n, :, head(c)].astype(F32)
            zw_out[n, :, head(c)] = total.astype(BF16)

            @pl.when(to_partner(n))
            def _(n=n):
                pin_copy(n, c).start()

    def relay(c):
        for n in range(planes):
            @pl.when(to_plane(n))
            def _(n=n):
                pin_copy(n, c).wait_recv()
                zw_out[n, :, head(c)] = (zw_out[n, :, head(c)].astype(F32) + pin[n, :, head(c)].astype(F32)).astype(BF16)
                tin_copy(n, c).start()

    def total_up(c):
        pin_copy(p, c).wait_recv()
        total = zw_out[p, :, head(c)].astype(F32) + pin[p, :, head(c)].astype(F32)
        for dk in range(1, planes // 2):
            k = lax.rem(group + dk, planes // 2)
            tin_came(k, c)
            total = total + tin[k, :, head(c)].astype(F32)
        for n in range(SPAN):
            fin_out[n, :, head(c)] = total[n * own_rows : (n + 1) * own_rows].astype(BF16)
        for d in (2, 3, 1):
            f_copy(d, c).start()

    def finish(c):
        for d in around:
            f_came(d, c)
        out_w[:, wide_head(r, c)] = fin_out[r, :, head(c)].astype(F32)
        for d in around:
            out_w[:, wide_head(peer[d], c)] = fin_in[peer[d], :, head(c)].astype(F32)

    def settle():
        kv[:, own_plane(r), :] = kv_in[:, :, quart(r)]
        for copy in own_copies:
            copy.wait()
        for h in range(2):
            up_came(1, h)
        turn(0)
        turn(1)

    def lift_on(h):
        up_came(2, h)
        up_copy(3, h).start()

    def lift_end():
        turn(2)
        for h in range(2):
            up_came(3, h)
        turn(3)

    def project_chip(c):
        project(c, 0)
        project(c, 1)

    def project_rest(c):
        project(c, 2)
        project(c, 3)

    forward_q(0)
    forward(0)
    pass_columns()
    lift_on(0)
    settle()
    attend(0)
    lift_on(1)
    project_chip(1)
    project_chip(0)
    lift_end()
    project_rest(0)
    forward(1)
    send_down(0)
    backward(0)
    weigh(0)
    project_chip(2)
    forward_q(1)
    forward(2)
    project_rest(2)
    project_rest(1)
    forward_q(2)
    attend(1)
    send_down(1)
    weigh(1)
    merge(0)
    attend(2)
    project_chip(3)
    forward(3)
    weigh(2)
    merge(1)
    relay(0)
    next_plane(0)
    send_down(2)
    return_kv(0)
    forward_q(3)
    attend(3)
    project_rest(3)
    relay(1)
    weigh(3)
    send_down(3)
    backward(2)
    backward(1)
    backward(3)
    merge(2)
    next_plane(1)
    return_kv(1)
    next_plane(2)
    total_up(0)
    total_up(1)
    relay(2)
    merge(3)
    next_plane(3)
    return_kv(2)
    relay(3)
    return_kv(3)
    total_up(2)
    finish(1)
    total_up(3)
    finish(2)
    finish(0)
    finish(3)
    for c in range(heads):
        for d in around:
            dq_came(d, c)
            dk_came(d, c)
            for copy in (kv_copy(d, c), q_copy(d, c), f_copy(d, c)):
                copy.wait_send()
        for j in range(SPAN):
            hand(j, lambda: own_dq(j, c).wait(), lambda: dq_copy(j, c).wait_send())
            hand(j, lambda: own_dk(j, c).wait(), lambda: dk_copy(j, c).wait_send())
        for df in range(1, fsdp):
            if by_side(c) is None:
                w_copy(df, c).wait_send()
            else:
                @pl.when(by_side(c))
                def _(c=c, df=df):
                    w_copy(df, c).wait_send()
                    wz_copy(df, c).wait_send()

            for n in range(planes):
                gx_copy(df, n, c).wait_send()
        for n in range(planes):
            @pl.when(to_partner(n))
            def _(n=n, c=c):
                pin_copy(n, c).wait_send()

            @pl.when(to_plane(n))
            def _(n=n, c=c):
                tin_copy(n, c).wait_send()

        @pl.when(not_last)
        def _(c=c):
            for d in range(SPAN):
                kz_copy(d, c).wait_send()

        @pl.when(not_first)
        def _(c=c):
            for d in range(SPAN):
                qz_copy(d, c).wait_send()
            ga_copy(c).wait_send()
            stats_copy(c).wait_send()

    for d in around:
        for h in range(2):
            up_copy(d, h).wait_send()


def hand_over_kernel(dq_in, kv_in, w_in, dq_out, kv_out, w_out):
    dq_out[...] = dq_in[...]
    w_out[...] = w_in[...]
    for n in range(2):
        kv_out[:, n, :] = kv_in[n]


def hand_over(dq, kv, w):
    toks, width = dq.shape
    vm = pl.BlockSpec(memory_space=pltpu.VMEM)
    return pl.pallas_call(
        hand_over_kernel,
        out_shape=(
            jax.ShapeDtypeStruct(dq.shape, dq.dtype),
            jax.ShapeDtypeStruct((toks, 2, width), kv.dtype),
            jax.ShapeDtypeStruct(w.shape, w.dtype),
        ),
        in_specs=[vm] * 3,
        out_specs=(vm,) * 3,
        name="hand_over",
    )(dq, kv, w)


def shards(queries, keys_values, upstream, out_weight):
    seqs, toks, width = queries.shape
    ctx, fsdp = lax.axis_size("ctx"), lax.axis_size("fsdp")
    planes = ctx // SPAN
    model = upstream.shape[2]
    own_rows = model // (ctx * fsdp)
    quarter = width // SPAN
    heads = quarter // HEAD_DIM
    group = SPAN * toks
    dma = pltpu.SemaphoreType.DMA
    any_spec = pl.BlockSpec(memory_space=pl.ANY)
    vm = pl.BlockSpec(memory_space=pltpu.VMEM)
    near = dma((SPAN, heads))
    sides = dma((fsdp, heads))
    levels = dma((planes, heads))
    parts = dma((fsdp, planes, heads))
    dq, out_kv, out_w = pl.pallas_call(
        functools.partial(layer_kernel, planes, fsdp),
        out_shape=(
            jax.ShapeDtypeStruct((toks, width), BF16),
            jax.ShapeDtypeStruct((2, toks, width), BF16),
            jax.ShapeDtypeStruct((own_rows, width), F32),
        ),
        in_specs=[any_spec] * 4,
        out_specs=(any_spec, any_spec, vm),
        scratch_shapes=[
            pltpu.VMEM((toks, 2, width), BF16),
            pltpu.VMEM((2, toks, width), BF16),
            pltpu.VMEM((group, quarter), BF16),
            pltpu.VMEM((2, 2 * group, quarter), BF16),
            pltpu.VMEM((group, model), BF16),
            pltpu.VMEM((model, group), BF16),
            pltpu.VMEM((model, quarter), BF16),
            pltpu.VMEM((group, quarter), BF16),
            pltpu.VMEM((group, quarter), BF16),
            pltpu.VMEM((heads * SPAN, toks, group + toks), BF16),
            pltpu.VMEM((SPAN, toks, group + toks), F32),
            pltpu.VMEM((group, quarter), BF16),
            pltpu.VMEM((2, group, quarter), F32),
            pltpu.VMEM((2, group, quarter), BF16),
            pltpu.VMEM((group, quarter), BF16),
            pltpu.VMEM((group, quarter), BF16),
            pltpu.VMEM((heads, 8, group), F32),
            pltpu.VMEM((heads, 8, group), F32),
            pltpu.VMEM((fsdp, planes, SPAN * own_rows, quarter), BF16),
            pltpu.VMEM((fsdp, planes, SPAN * own_rows, quarter), BF16),
            pltpu.VMEM((planes, SPAN * own_rows, quarter), BF16),
            pltpu.VMEM((planes, SPAN * own_rows, quarter), BF16),
            pltpu.VMEM((planes // 2, SPAN * own_rows, quarter), BF16),
            pltpu.VMEM((SPAN, own_rows, quarter), BF16),
            pltpu.VMEM((SPAN, own_rows, quarter), BF16),
            dma((4,)), near, near, near, near, dma((SPAN, 2)), dma((SPAN, 2)), sides, sides, sides, sides, near, near,
            near, near, near, near, near, near, dma((heads,)), dma((heads,)), dma((heads,)), dma((heads,)), parts, parts, levels, levels, levels, dma((planes // 2, heads)), near, near,
        ],
        compiler_params=pltpu.CompilerParams(collective_id=0, has_side_effects=True),
        name="layer",
    )(queries[0], keys_values[0], upstream[0], out_weight)
    dq, out_kv, out_w = hand_over(dq, out_kv, out_w)
    return dq[None], out_kv[None], out_w


def solution(mesh):
    return jax.shard_map(
        shards,
        mesh=mesh,
        in_specs=(
            P("fsdp", "ctx", None),
            P("fsdp", "ctx", None, None),
            P("fsdp", "ctx", None),
            P("fsdp", None),
        ),
        out_specs=(P("fsdp", "ctx", None), P("fsdp", "ctx", None, None), P(("ctx", "fsdp"), None)),
        check_vma=False,
    )
```

```python
import functools

import jax
import jax.numpy as jnp
from jax import lax
from jax.experimental import pallas as pl
from jax.experimental.pallas import tpu as pltpu
from jax.sharding import PartitionSpec as P

HEAD_DIM = 128
SPAN = 4
NEGATIVE = -1e30
F32 = jnp.float32
BF16 = jnp.bfloat16
NT = (((1,), (1,)), ((), ()))
TN = (((0,), (0,)), ((), ()))


def remote(src, dst, send, recv, device):
    return pltpu.make_async_remote_copy(
        src_ref=src, dst_ref=dst, send_sem=send, recv_sem=recv, device_id=device, device_id_type=pl.DeviceIdType.MESH
    )


def layer_kernel(
    planes, fsdp,
    q_in, kv_pairs, up_in, weight,
    dq_out, kv_out, out_w,
    kv_raw, kv_in, q, kv, up, up_t, w, ga, att, low, bias, dq, dkv, dsum, q_next, ga_next, stats, stats_next,
    gw_out, gw_in, zw_out, pin, tin, fin_out, fin_in,
    own_sem, kv_s, kv_r, q_s, q_r, u_s, u_r, w_s, w_r, wz_s, wz_r, kz_s, kz_r,
    dq_s, dq_r, dk_s, dk_r, qz_s, qz_r, gz_s, gz_r, st_s, st_r, gx_s, gx_r, pin_s, pin_r, tin_s, tin_r, f_s, f_r,
):
    toks = q_in.shape[0]
    depth = weight.shape[0]
    width = weight.shape[1]
    width_up = up_in.shape[1] // 2
    quarter = width // SPAN
    heads = quarter // HEAD_DIM
    plane_toks = SPAN * toks
    keys = plane_toks + toks
    own_rows = out_w.shape[0]
    plane_rows = SPAN * own_rows
    inv_root = HEAD_DIM ** (-0.5)

    me = lax.axis_index("ctx")
    f = lax.axis_index("fsdp")
    p = lax.div(me, SPAN)
    r = lax.rem(me, SPAN)
    mate = r + 1 - 2 * lax.rem(r, 2)
    peer = [r, mate, lax.rem(r + 2, SPAN), lax.rem(mate + 2, SPAN)]
    not_first = p > 0
    not_last = p < planes - 1

    def dev(p_, r_, f_):
        return {"ctx": p_ * SPAN + r_, "fsdp": f_}

    def near(d):
        return dev(p, peer[d], f)

    def side(df):
        return lax.rem(f + df, fsdp)

    def level(dp):
        return lax.rem(p + dp, planes)

    def rows(i):
        return pl.ds(pl.multiple_of(i * toks, toks), toks)

    def own_plane(i):
        return pl.ds(pl.multiple_of(plane_toks + i * toks, toks), toks)

    def head(c):
        return pl.ds(c * HEAD_DIM, HEAD_DIM)

    def wide_head(i, c):
        return pl.ds(pl.multiple_of(i * quarter + c * HEAD_DIM, HEAD_DIM), HEAD_DIM)

    def quart(i):
        return pl.ds(pl.multiple_of(i * quarter, quarter), quarter)

    def w_rows(i):
        return pl.ds(pl.multiple_of(i * depth, depth), depth)

    pairs_copy = pltpu.make_async_copy(kv_pairs, kv_raw, own_sem.at[0])
    pairs_copy.start()
    own_copies = [
        pltpu.make_async_copy(q_in.at[:, quart(r)], q.at[rows(r), :], own_sem.at[1]),
        pltpu.make_async_copy(up_in, up.at[rows(r), :], own_sem.at[2]),
        pltpu.make_async_copy(weight.at[:, quart(r)], w.at[w_rows(f), :], own_sem.at[3]),
    ]
    for copy in own_copies:
        copy.start()

    sem = pltpu.get_barrier_semaphore()
    targets = [near(d) for d in range(1, SPAN)]
    targets += [dev(p, r, side(df)) for df in range(1, fsdp)]
    targets += [dev(level(dp), r, f) for dp in range(1, planes)]
    for target in targets:
        pl.semaphore_signal(sem, inc=1, device_id=target, device_id_type=pl.DeviceIdType.MESH)
    pairs_copy.wait()
    for n in range(2):
        kv_in[n] = kv_raw[:, n, :]
    pl.semaphore_wait(sem, len(targets))

    def kv_copy(d, c):
        return remote(kv_in.at[:, :, wide_head(peer[d], c)], kv.at[:, own_plane(r), head(c)], kv_s.at[d, c], kv_r.at[d, c], near(d))

    def kv_came(d, c):
        here = kv.at[:, own_plane(peer[d]), head(c)]
        remote(here, here, kv_s.at[d, c], kv_r.at[d, c], near(d)).wait_recv()

    def q_copy(d, c):
        return remote(q_in.at[:, wide_head(peer[d], c)], q.at[rows(r), head(c)], q_s.at[d, c], q_r.at[d, c], near(d))

    def q_came(d, c):
        here = q.at[rows(peer[d]), head(c)]
        remote(here, here, q_s.at[d, c], q_r.at[d, c], near(d)).wait_recv()

    def up_copy(d, h):
        cols = slice(h * width_up, (h + 1) * width_up)
        if d == 3:
            here = up.at[rows(peer[2]), cols]
            return remote(here, here, u_s.at[3, h], u_r.at[3, h], near(1))
        return remote(up_in.at[:, cols], up.at[rows(r), cols], u_s.at[d, h], u_r.at[d, h], near(d))

    def up_came(d, h):
        here = up.at[rows(peer[d]), h * width_up : (h + 1) * width_up]
        remote(here, here, u_s.at[d, h], u_r.at[d, h], near(d)).wait_recv()

    def w_copy(df, c):
        return remote(
            weight.at[:, wide_head(r, c)], w.at[w_rows(f), head(c)], w_s.at[df, c], w_r.at[fsdp - df, c], dev(p, r, side(df))
        )

    def w_came(df, c):
        here = w.at[w_rows(side(df)), head(c)]
        remote(here, here, w_s.at[df, c], w_r.at[df, c], dev(p, r, side(df))).wait_recv()

    lower = lax.rem(p, 2) == 0
    upper = jnp.logical_not(lower)
    partner = dev(p + 1 - 2 * lax.rem(p, 2), r, f)

    def wz_copy(df, c):
        here = w.at[w_rows(side(df)), head(c)]
        return remote(here, here, wz_s.at[df, c], wz_r.at[df, c], partner)

    def by_side(c):
        if c == heads - 2:
            return lower
        if c == heads - 1:
            return upper
        return None

    def kz_copy(d, c):
        src = kv_in.at[:, :, wide_head(r, c)] if d == 0 else kv.at[:, own_plane(peer[d]), head(c)]
        return remote(src, kv.at[:, rows(peer[d]), head(c)], kz_s.at[d, c], kz_r.at[d, c], dev(p + 1, r, f))

    def block_head(ref, lead, j, c):
        return ref.at[lead + (slice(j * toks, (j + 1) * toks), head(c))]

    def dq_copy(j, c):
        return remote(block_head(dq, (), j, c), dq_out.at[:, wide_head(r, c)], dq_s.at[j, c], dq_r.at[r, c], dev(p, j, f))

    def dq_came(d, c):
        here = dq_out.at[:, wide_head(peer[d], c)]
        remote(here, here, dq_s.at[0, c], dq_r.at[peer[d], c], near(d)).wait_recv()

    def own_dq(j, c):
        return pltpu.make_async_copy(block_head(dq, (), j, c), dq_out.at[:, wide_head(r, c)], dq_s.at[j, c])

    def qz_copy(d, c):
        src = q_in.at[:, wide_head(r, c)] if d == 0 else q.at[rows(peer[d]), head(c)]
        return remote(src, q_next.at[rows(peer[d]), head(c)], qz_s.at[d, c], qz_r.at[d, c], dev(p - 1, r, f))

    def ga_copy(c):
        return remote(ga.at[:, head(c)], ga_next.at[:, head(c)], gz_s.at[c], gz_r.at[c], dev(p - 1, r, f))

    def stats_copy(c):
        return remote(stats.at[c], stats_next.at[c], st_s.at[c], st_r.at[c], dev(p - 1, r, f))

    def dk_copy(j, c):
        return remote(block_head(dsum, (slice(None),), j, c), kv_out.at[:, :, wide_head(r, c)], dk_s.at[j, c], dk_r.at[r, c], dev(p, j, f))

    def dk_came(d, c):
        here = kv_out.at[:, :, wide_head(peer[d], c)]
        remote(here, here, dk_s.at[0, c], dk_r.at[peer[d], c], near(d)).wait_recv()

    def own_dk(j, c):
        return pltpu.make_async_copy(block_head(dsum, (slice(None),), j, c), kv_out.at[:, :, wide_head(r, c)], dk_s.at[j, c])

    def hand(j, own, other):
        @pl.when(r == j)
        def _():
            own()

        @pl.when(r != j)
        def _():
            other()

    def gx_copy(df, n, c):
        return remote(
            gw_out.at[side(df), n, :, head(c)], gw_in.at[fsdp - df, n, :, head(c)], gx_s.at[df, n, c], gx_r.at[fsdp - df, n, c],
            dev(p, r, side(df)),
        )

    def gx_came(df, n, c):
        here = gw_in.at[df, n, :, head(c)]
        remote(here, here, gx_s.at[df, n, c], gx_r.at[df, n, c], dev(p, r, side(df))).wait_recv()

    group = lax.div(p, 2)
    far_first = [lax.rem(2 * (group + 1) + i, planes) for i in range(planes - 2)] + [p + 1 - 2 * lax.rem(p, 2), p]

    def to_partner(n):
        return jnp.logical_or(jnp.logical_and(lower, n > p), jnp.logical_and(upper, n < p))

    def to_plane(n):
        return jnp.logical_or(jnp.logical_and(lower, n < p), jnp.logical_and(upper, n > p))

    def pin_copy(n, c):
        return remote(zw_out.at[n, :, head(c)], pin.at[n, :, head(c)], pin_s.at[n, c], pin_r.at[n, c], partner)

    def tin_copy(n, c):
        return remote(zw_out.at[n, :, head(c)], tin.at[group, :, head(c)], tin_s.at[n, c], tin_r.at[group, c], dev(n, r, f))

    def tin_came(k, c):
        here = tin.at[k, :, head(c)]
        remote(here, here, tin_s.at[0, c], tin_r.at[k, c], partner).wait_recv()

    def f_copy(d, c):
        return remote(fin_out.at[peer[d], :, head(c)], fin_in.at[r, :, head(c)], f_s.at[d, c], f_r.at[d, c], near(d))

    def f_came(d, c):
        here = fin_in.at[peer[d], :, head(c)]
        remote(here, here, f_s.at[d, c], f_r.at[d, c], near(d)).wait_recv()

    around = range(1, SPAN)

    def spread_kv(c):
        for d in around:
            kv_copy(d, c).start()

    def spread_q(c):
        for d in around:
            q_copy(d, c).start()

        @pl.when(not_first)
        def _():
            qz_copy(0, c).start()

    def halo(c):
        @pl.when(not_last)
        def _():
            kz_copy(0, c).start()

    def columns(c):
        def go():
            for df in range(1, fsdp):
                w_copy(df, c).start()

        if by_side(c) is None:
            go()
        else:
            pl.when(by_side(c))(go)

    def pass_columns():
        for c in (heads - 2, heads - 1):
            @pl.when(by_side(c))
            def _(c=c):
                for df in range(1, fsdp):
                    w_came(df, c)
                    wz_copy(df, c).start()

    def lift():
        for h in range(2):
            up_copy(2, h).start()
        for h in range(2):
            up_copy(1, h).start()

    halo(0)
    halo(1)
    spread_kv(0)
    spread_q(0)
    columns(0)
    columns(2)
    spread_q(1)
    columns(3)
    lift()
    spread_q(2)
    spread_kv(1)
    halo(2)
    spread_q(3)
    halo(3)
    spread_kv(2)
    columns(1)
    spread_kv(3)
    row = lax.broadcasted_iota(jnp.int32, (toks, keys), 0)
    col = lax.broadcasted_iota(jnp.int32, (toks, keys), 1)
    for b in range(SPAN):
        first = jnp.where(not_first, 0, plane_toks - b * toks)
        bias[b] = jnp.where((col > row) & (col <= row + plane_toks) & (col >= first), 0.0, NEGATIVE)
    dkv[...] = jnp.zeros(dkv.shape, F32)
    stats[...] = jnp.zeros(stats.shape, F32)

    @pl.when(p == 0)
    def _():
        kv[:, :plane_toks] = jnp.zeros((2, plane_toks, quarter), BF16)

    def forward(c):
        for d in around:
            kv_came(d, c)

            @pl.when(not_last)
            def _(d=d):
                kz_copy(d, c).start()

    def forward_q(c):
        for d in around:
            q_came(d, c)

            @pl.when(not_first)
            def _(d=d):
                qz_copy(d, c).start()

    diagonal = lax.broadcasted_iota(jnp.int32, (toks, toks), 0) == lax.broadcasted_iota(jnp.int32, (toks, toks), 1)

    def as_row(column):
        return jnp.sum(jnp.where(diagonal, column, 0.0), axis=0, keepdims=True)

    def window(b):
        return pl.ds(b * toks, keys)

    def attend(c):
        @pl.when(not_first)
        def _():
            for d in range(SPAN):
                here = kv.at[:, rows(peer[d]), head(c)]
                remote(here, here, kz_s.at[d, c], kz_r.at[d, c], near(1)).wait_recv()

        for b in range(SPAN):
            block = pl.ds(b * toks, toks)
            scores = lax.dot_general(q[block, head(c)], kv[0, window(b), head(c)], NT, preferred_element_type=F32) * inv_root + bias[b]
            top = jnp.max(scores, axis=-1, keepdims=True)
            lifted = jnp.exp(scores - top)
            mass = jnp.sum(lifted, axis=-1, keepdims=True)
            stats[c, 0:1, block] = as_row(top + jnp.log(mass))
            prob = (lifted * (1.0 / mass)).astype(BF16)
            low[c * SPAN + b] = prob
            att[block, head(c)] = jnp.dot(prob, kv[1, window(b), head(c)], preferred_element_type=F32).astype(BF16)

    def center_of(block, c):
        return jnp.sum(ga[block, head(c)].astype(F32) * att[block, head(c)].astype(F32), axis=-1, keepdims=True)

    def send_down(c):
        @pl.when(not_first)
        def _():
            for b in range(SPAN):
                block = pl.ds(b * toks, toks)
                stats[c, 1:2, block] = as_row(center_of(block, c))
            ga_copy(c).start()
            stats_copy(c).start()

    def backward(c):
        for b in range(SPAN):
            block = pl.ds(b * toks, toks)
            g = ga[block, head(c)]
            prob = low[c * SPAN + b]
            k = kv[0, window(b), head(c)]
            products = lax.dot_general(g, kv[1, window(b), head(c)], NT, preferred_element_type=F32)
            ds = (prob.astype(F32) * (products - center_of(block, c))).astype(BF16)
            dq[block, head(c)] = (jnp.dot(ds, k, preferred_element_type=F32) * inv_root).astype(BF16)
            seen = slice(plane_toks - b * toks, keys)
            mine = slice(0, (b + 1) * toks)
            dkv[0, mine, head(c)] += lax.dot_general(ds[:, seen], q[block, head(c)], TN, preferred_element_type=F32) * inv_root
            dkv[1, mine, head(c)] += lax.dot_general(prob[:, seen], g, TN, preferred_element_type=F32)
        for j in range(SPAN):
            hand(j, lambda: own_dq(j, c).start(), lambda: dq_copy(j, c).start())

    def next_plane(c):
        @pl.when(not_last)
        def _():
            for d in range(SPAN):
                here = q_next.at[rows(peer[d]), head(c)]
                remote(here, here, qz_s.at[d, c], qz_r.at[d, c], near(1)).wait_recv()
            ga_copy(c).wait_recv()
            stats_copy(c).wait_recv()
            for b in range(SPAN):
                block = pl.ds(b * toks, toks)
                count = plane_toks - b * toks
                mine = slice(b * toks, plane_toks)
                seen = slice(plane_toks + b * toks, 2 * plane_toks)
                shape = (count, toks)
                visible = lax.broadcasted_iota(jnp.int32, shape, 0) > lax.broadcasted_iota(jnp.int32, shape, 1)
                qn, gn = q_next[block, head(c)], ga_next[block, head(c)]
                scores = lax.dot_general(kv[0, seen, head(c)], qn, NT, preferred_element_type=F32) * inv_root
                prob = jnp.exp(jnp.where(visible, scores - stats_next[c, 0:1, block], NEGATIVE))
                products = lax.dot_general(kv[1, seen, head(c)], gn, NT, preferred_element_type=F32)
                ds = (prob * (products - stats_next[c, 1:2, block])).astype(BF16)
                dkv[0, mine, head(c)] += jnp.dot(ds, qn, preferred_element_type=F32) * inv_root
                dkv[1, mine, head(c)] += jnp.dot(prob.astype(BF16), gn, preferred_element_type=F32)

    def return_kv(c):
        dsum[:, :, head(c)] = dkv[:, :, head(c)].astype(BF16)
        for j in range(SPAN):
            hand(j, lambda: own_dk(j, c).start(), lambda: dk_copy(j, c).start())

    def project(c, d):
        if d == 0:
            for df in range(1, fsdp):
                if by_side(c) is None:
                    w_came(df, c)
                else:
                    pl.when(jnp.logical_not(by_side(c)))(lambda df=df: wz_copy(df, c).wait_recv())
        ga[rows(peer[d]), head(c)] = jnp.dot(up[rows(peer[d]), :], w[:, head(c)], preferred_element_type=F32).astype(BF16)

    def turn(d):
        up_t[:, rows(peer[d])] = up[rows(peer[d]), :].T

    tile = up_in.shape[1] // planes

    def weigh(c):
        for n in far_first:
            rows_n = pl.ds(pl.multiple_of(n * tile, tile), tile)
            value = jnp.dot(up_t[rows_n, :], att[:, head(c)], preferred_element_type=F32)
            value = value.reshape(SPAN, fsdp, own_rows, HEAD_DIM)
            for i in range(fsdp):
                gw_out[i, n, :, head(c)] = value[:, i].reshape(plane_rows, HEAD_DIM).astype(BF16)
            for df in range(1, fsdp):
                gx_copy(df, n, c).start()

    def merge(c):
        for n in far_first:
            total = gw_out[f, n, :, head(c)].astype(F32)
            for df in range(1, fsdp):
                gx_came(df, n, c)
                total = total + gw_in[df, n, :, head(c)].astype(F32)
            zw_out[n, :, head(c)] = total.astype(BF16)

            @pl.when(to_partner(n))
            def _(n=n):
                pin_copy(n, c).start()

    def relay(c):
        for n in range(planes):
            @pl.when(to_plane(n))
            def _(n=n):
                pin_copy(n, c).wait_recv()
                zw_out[n, :, head(c)] = (zw_out[n, :, head(c)].astype(F32) + pin[n, :, head(c)].astype(F32)).astype(BF16)
                tin_copy(n, c).start()

    def total_up(c):
        pin_copy(p, c).wait_recv()
        total = zw_out[p, :, head(c)].astype(F32) + pin[p, :, head(c)].astype(F32)
        for dk in range(1, planes // 2):
            k = lax.rem(group + dk, planes // 2)
            tin_came(k, c)
            total = total + tin[k, :, head(c)].astype(F32)
        for n in range(SPAN):
            fin_out[n, :, head(c)] = total[n * own_rows : (n + 1) * own_rows].astype(BF16)
        for d in (2, 3, 1):
            f_copy(d, c).start()

    def finish(c):
        for d in around:
            f_came(d, c)
        out_w[:, wide_head(r, c)] = fin_out[r, :, head(c)].astype(F32)
        for d in around:
            out_w[:, wide_head(peer[d], c)] = fin_in[peer[d], :, head(c)].astype(F32)

    def settle():
        kv[:, own_plane(r), :] = kv_in[:, :, quart(r)]
        for copy in own_copies:
            copy.wait()
        for h in range(2):
            up_came(1, h)
        turn(0)
        turn(1)

    def lift_on(h):
        up_came(2, h)
        up_copy(3, h).start()

    def lift_end():
        turn(2)
        for h in range(2):
            up_came(3, h)
        turn(3)

    def project_chip(c):
        project(c, 0)
        project(c, 1)

    def project_rest(c):
        project(c, 2)
        project(c, 3)

    forward(0)
    settle()
    forward_q(1)
    project_chip(0)
    forward_q(0)
    pass_columns()
    attend(0)
    lift_on(0)
    lift_on(1)
    forward_q(2)
    lift_end()
    project_rest(0)
    weigh(0)
    project_chip(2)
    send_down(0)
    project_chip(1)
    forward(1)
    project_chip(3)
    project_rest(2)
    backward(0)
    forward_q(3)
    forward(2)
    project_rest(1)
    merge(0)
    attend(1)
    send_down(1)
    weigh(1)
    backward(1)
    forward(3)
    attend(2)
    send_down(2)
    weigh(2)
    relay(0)
    next_plane(0)
    merge(1)
    backward(2)
    next_plane(2)
    attend(3)
    total_up(0)
    merge(2)
    project_rest(3)
    return_kv(2)
    relay(1)
    weigh(3)
    finish(0)
    return_kv(0)
    send_down(3)
    total_up(1)
    next_plane(1)
    return_kv(1)
    relay(2)
    merge(3)
    backward(3)
    next_plane(3)
    relay(3)
    return_kv(3)
    total_up(2)
    finish(1)
    total_up(3)
    finish(2)
    finish(3)
    for c in range(heads):
        for d in around:
            dq_came(d, c)
            dk_came(d, c)
            for copy in (kv_copy(d, c), q_copy(d, c), f_copy(d, c)):
                copy.wait_send()
        for j in range(SPAN):
            hand(j, lambda: own_dq(j, c).wait(), lambda: dq_copy(j, c).wait_send())
            hand(j, lambda: own_dk(j, c).wait(), lambda: dk_copy(j, c).wait_send())
        for df in range(1, fsdp):
            if by_side(c) is None:
                w_copy(df, c).wait_send()
            else:
                @pl.when(by_side(c))
                def _(c=c, df=df):
                    w_copy(df, c).wait_send()
                    wz_copy(df, c).wait_send()

            for n in range(planes):
                gx_copy(df, n, c).wait_send()
        for n in range(planes):
            @pl.when(to_partner(n))
            def _(n=n, c=c):
                pin_copy(n, c).wait_send()

            @pl.when(to_plane(n))
            def _(n=n, c=c):
                tin_copy(n, c).wait_send()

        @pl.when(not_last)
        def _(c=c):
            for d in range(SPAN):
                kz_copy(d, c).wait_send()

        @pl.when(not_first)
        def _(c=c):
            for d in range(SPAN):
                qz_copy(d, c).wait_send()
            ga_copy(c).wait_send()
            stats_copy(c).wait_send()

    for d in around:
        for h in range(2):
            up_copy(d, h).wait_send()


def hand_over_kernel(dq_in, kv_in, w_in, dq_out, kv_out, w_out):
    dq_out[...] = dq_in[...]
    w_out[...] = w_in[...]
    for n in range(2):
        kv_out[:, n, :] = kv_in[n]


def hand_over(dq, kv, w):
    toks, width = dq.shape
    steps = 2
    part = toks // steps
    whole = pl.BlockSpec(w.shape, lambda i: (0, 0))
    piece = pl.BlockSpec((part, width), lambda i: (i, 0))
    return pl.pallas_call(
        hand_over_kernel,
        grid=(steps,),
        out_shape=(
            jax.ShapeDtypeStruct(dq.shape, dq.dtype),
            jax.ShapeDtypeStruct((toks, 2, width), kv.dtype),
            jax.ShapeDtypeStruct(w.shape, w.dtype),
        ),
        in_specs=[piece, pl.BlockSpec((2, part, width), lambda i: (0, i, 0)), whole],
        out_specs=(piece, pl.BlockSpec((part, 2, width), lambda i: (i, 0, 0)), whole),
        name="hand_over",
    )(dq, kv, w)


def shards(queries, keys_values, upstream, out_weight):
    seqs, toks, width = queries.shape
    ctx, fsdp = lax.axis_size("ctx"), lax.axis_size("fsdp")
    planes = ctx // SPAN
    model = upstream.shape[2]
    own_rows = model // (ctx * fsdp)
    quarter = width // SPAN
    heads = quarter // HEAD_DIM
    group = SPAN * toks
    dma = pltpu.SemaphoreType.DMA
    any_spec = pl.BlockSpec(memory_space=pl.ANY)
    vm = pl.BlockSpec(memory_space=pltpu.VMEM)
    near = dma((SPAN, heads))
    sides = dma((fsdp, heads))
    levels = dma((planes, heads))
    parts = dma((fsdp, planes, heads))
    dq, out_kv, out_w = pl.pallas_call(
        functools.partial(layer_kernel, planes, fsdp),
        out_shape=(
            jax.ShapeDtypeStruct((toks, width), BF16),
            jax.ShapeDtypeStruct((2, toks, width), BF16),
            jax.ShapeDtypeStruct((own_rows, width), F32),
        ),
        in_specs=[any_spec] * 4,
        out_specs=(any_spec, any_spec, vm),
        scratch_shapes=[
            pltpu.VMEM((toks, 2, width), BF16),
            pltpu.VMEM((2, toks, width), BF16),
            pltpu.VMEM((group, quarter), BF16),
            pltpu.VMEM((2, 2 * group, quarter), BF16),
            pltpu.VMEM((group, model), BF16),
            pltpu.VMEM((model, group), BF16),
            pltpu.VMEM((model, quarter), BF16),
            pltpu.VMEM((group, quarter), BF16),
            pltpu.VMEM((group, quarter), BF16),
            pltpu.VMEM((heads * SPAN, toks, group + toks), BF16),
            pltpu.VMEM((SPAN, toks, group + toks), F32),
            pltpu.VMEM((group, quarter), BF16),
            pltpu.VMEM((2, group, quarter), F32),
            pltpu.VMEM((2, group, quarter), BF16),
            pltpu.VMEM((group, quarter), BF16),
            pltpu.VMEM((group, quarter), BF16),
            pltpu.VMEM((heads, 8, group), F32),
            pltpu.VMEM((heads, 8, group), F32),
            pltpu.VMEM((fsdp, planes, SPAN * own_rows, quarter), BF16),
            pltpu.VMEM((fsdp, planes, SPAN * own_rows, quarter), BF16),
            pltpu.VMEM((planes, SPAN * own_rows, quarter), BF16),
            pltpu.VMEM((planes, SPAN * own_rows, quarter), BF16),
            pltpu.VMEM((planes // 2, SPAN * own_rows, quarter), BF16),
            pltpu.VMEM((SPAN, own_rows, quarter), BF16),
            pltpu.VMEM((SPAN, own_rows, quarter), BF16),
            dma((4,)), near, near, near, near, dma((SPAN, 2)), dma((SPAN, 2)), sides, sides, sides, sides, near, near,
            near, near, near, near, near, near, dma((heads,)), dma((heads,)), dma((heads,)), dma((heads,)), parts, parts, levels, levels, levels, dma((planes // 2, heads)), near, near,
        ],
        compiler_params=pltpu.CompilerParams(collective_id=0, has_side_effects=True),
        name="layer",
    )(queries[0], keys_values[0], upstream[0], out_weight)
    dq, out_kv, out_w = hand_over(dq, out_kv, out_w)
    return dq[None], out_kv[None], out_w


def solution(mesh):
    return jax.shard_map(
        shards,
        mesh=mesh,
        in_specs=(
            P("fsdp", "ctx", None),
            P("fsdp", "ctx", None, None),
            P("fsdp", "ctx", None),
            P("fsdp", None),
        ),
        out_specs=(P("fsdp", "ctx", None), P("fsdp", "ctx", None, None), P(("ctx", "fsdp"), None)),
        check_vma=False,
    )
```

```python
import functools

import jax
import jax.numpy as jnp
from jax import lax
from jax.experimental import pallas as pl
from jax.experimental.pallas import tpu as pltpu
from jax.sharding import PartitionSpec as P

HEAD_DIM = 128
SPAN = 4
NEGATIVE = -1e30
F32 = jnp.float32
BF16 = jnp.bfloat16
NT = (((1,), (1,)), ((), ()))
TN = (((0,), (0,)), ((), ()))


def remote(src, dst, send, recv, device):
    return pltpu.make_async_remote_copy(
        src_ref=src, dst_ref=dst, send_sem=send, recv_sem=recv, device_id=device, device_id_type=pl.DeviceIdType.MESH
    )


def layer_kernel(
    planes, fsdp,
    q_in, kv_pairs, up_in, weight,
    dq_out, kv_out, out_w,
    kv_raw, kv_in, q, kv, up, up_t, w, ga, att, low, bias, dq, dkv, dsum, q_next, ga_next, stats, stats_next,
    gw_out, gw_in, zw_out, pin, tin, fin_out, fin_in,
    own_sem, kv_s, kv_r, q_s, q_r, u_s, u_r, w_s, w_r, wz_s, wz_r, kz_s, kz_r,
    dq_s, dq_r, dk_s, dk_r, qz_s, qz_r, gz_s, gz_r, st_s, st_r, gx_s, gx_r, pin_s, pin_r, tin_s, tin_r, f_s, f_r,
):
    toks = q_in.shape[0]
    depth = weight.shape[0]
    width = weight.shape[1]
    width_up = up_in.shape[1] // 2
    quarter = width // SPAN
    heads = quarter // HEAD_DIM
    plane_toks = SPAN * toks
    keys = plane_toks + toks
    own_rows = out_w.shape[0]
    plane_rows = SPAN * own_rows
    inv_root = HEAD_DIM ** (-0.5)

    me = lax.axis_index("ctx")
    f = lax.axis_index("fsdp")
    p = lax.div(me, SPAN)
    r = lax.rem(me, SPAN)
    mate = r + 1 - 2 * lax.rem(r, 2)
    peer = [r, mate, lax.rem(r + 2, SPAN), lax.rem(mate + 2, SPAN)]
    not_first = p > 0
    not_last = p < planes - 1

    def dev(p_, r_, f_):
        return {"ctx": p_ * SPAN + r_, "fsdp": f_}

    def near(d):
        return dev(p, peer[d], f)

    def side(df):
        return lax.rem(f + df, fsdp)

    def level(dp):
        return lax.rem(p + dp, planes)

    def rows(i):
        return pl.ds(pl.multiple_of(i * toks, toks), toks)

    def own_plane(i):
        return pl.ds(pl.multiple_of(plane_toks + i * toks, toks), toks)

    def head(c):
        return pl.ds(c * HEAD_DIM, HEAD_DIM)

    def wide_head(i, c):
        return pl.ds(pl.multiple_of(i * quarter + c * HEAD_DIM, HEAD_DIM), HEAD_DIM)

    def quart(i):
        return pl.ds(pl.multiple_of(i * quarter, quarter), quarter)

    def w_rows(i):
        return pl.ds(pl.multiple_of(i * depth, depth), depth)

    pairs_copy = pltpu.make_async_copy(kv_pairs, kv_raw, own_sem.at[0])
    pairs_copy.start()
    own_copies = [
        pltpu.make_async_copy(q_in.at[:, quart(r)], q.at[rows(r), :], own_sem.at[1]),
        pltpu.make_async_copy(up_in, up.at[rows(r), :], own_sem.at[2]),
        pltpu.make_async_copy(weight.at[:, quart(r)], w.at[w_rows(f), :], own_sem.at[3]),
    ]
    for copy in own_copies:
        copy.start()

    sem = pltpu.get_barrier_semaphore()
    targets = [near(d) for d in range(1, SPAN)]
    targets += [dev(p, r, side(df)) for df in range(1, fsdp)]
    targets += [dev(level(dp), r, f) for dp in range(1, planes)]
    for target in targets:
        pl.semaphore_signal(sem, inc=1, device_id=target, device_id_type=pl.DeviceIdType.MESH)
    pairs_copy.wait()
    for n in range(2):
        kv_in[n] = kv_raw[:, n, :]
    pl.semaphore_wait(sem, len(targets))

    def kv_copy(d, c):
        return remote(kv_in.at[:, :, wide_head(peer[d], c)], kv.at[:, own_plane(r), head(c)], kv_s.at[d, c], kv_r.at[d, c], near(d))

    def kv_came(d, c):
        here = kv.at[:, own_plane(peer[d]), head(c)]
        remote(here, here, kv_s.at[d, c], kv_r.at[d, c], near(d)).wait_recv()

    def q_copy(d, c):
        return remote(q_in.at[:, wide_head(peer[d], c)], q.at[rows(r), head(c)], q_s.at[d, c], q_r.at[d, c], near(d))

    def q_came(d, c):
        here = q.at[rows(peer[d]), head(c)]
        remote(here, here, q_s.at[d, c], q_r.at[d, c], near(d)).wait_recv()

    def up_copy(d, h):
        cols = slice(h * width_up, (h + 1) * width_up)
        if d == 3:
            here = up.at[rows(peer[2]), cols]
            return remote(here, here, u_s.at[3, h], u_r.at[3, h], near(1))
        return remote(up_in.at[:, cols], up.at[rows(r), cols], u_s.at[d, h], u_r.at[d, h], near(d))

    def up_came(d, h):
        here = up.at[rows(peer[d]), h * width_up : (h + 1) * width_up]
        remote(here, here, u_s.at[d, h], u_r.at[d, h], near(d)).wait_recv()

    def w_copy(df, c):
        return remote(
            weight.at[:, wide_head(r, c)], w.at[w_rows(f), head(c)], w_s.at[df, c], w_r.at[fsdp - df, c], dev(p, r, side(df))
        )

    def w_came(df, c):
        here = w.at[w_rows(side(df)), head(c)]
        remote(here, here, w_s.at[df, c], w_r.at[df, c], dev(p, r, side(df))).wait_recv()

    lower = lax.rem(p, 2) == 0
    upper = jnp.logical_not(lower)
    partner = dev(p + 1 - 2 * lax.rem(p, 2), r, f)

    def wz_copy(df, c):
        here = w.at[w_rows(side(df)), head(c)]
        return remote(here, here, wz_s.at[df, c], wz_r.at[df, c], partner)

    def by_side(c):
        if c == heads - 2:
            return lower
        if c == heads - 1:
            return upper
        return None

    def kz_copy(d, c):
        src = kv_in.at[:, :, wide_head(r, c)] if d == 0 else kv.at[:, own_plane(peer[d]), head(c)]
        return remote(src, kv.at[:, rows(peer[d]), head(c)], kz_s.at[d, c], kz_r.at[d, c], dev(p + 1, r, f))

    def block_head(ref, lead, j, c):
        return ref.at[lead + (slice(j * toks, (j + 1) * toks), head(c))]

    def dq_copy(j, c):
        return remote(block_head(dq, (), j, c), dq_out.at[:, wide_head(r, c)], dq_s.at[j, c], dq_r.at[r, c], dev(p, j, f))

    def dq_came(d, c):
        here = dq_out.at[:, wide_head(peer[d], c)]
        remote(here, here, dq_s.at[0, c], dq_r.at[peer[d], c], near(d)).wait_recv()

    def own_dq(j, c):
        return pltpu.make_async_copy(block_head(dq, (), j, c), dq_out.at[:, wide_head(r, c)], dq_s.at[j, c])

    def qz_copy(d, c):
        src = q_in.at[:, wide_head(r, c)] if d == 0 else q.at[rows(peer[d]), head(c)]
        return remote(src, q_next.at[rows(peer[d]), head(c)], qz_s.at[d, c], qz_r.at[d, c], dev(p - 1, r, f))

    def ga_copy(c):
        return remote(ga.at[:, head(c)], ga_next.at[:, head(c)], gz_s.at[c], gz_r.at[c], dev(p - 1, r, f))

    def stats_copy(c):
        return remote(stats.at[c], stats_next.at[c], st_s.at[c], st_r.at[c], dev(p - 1, r, f))

    def dk_copy(j, c):
        return remote(block_head(dsum, (slice(None),), j, c), kv_out.at[:, :, wide_head(r, c)], dk_s.at[j, c], dk_r.at[r, c], dev(p, j, f))

    def dk_came(d, c):
        here = kv_out.at[:, :, wide_head(peer[d], c)]
        remote(here, here, dk_s.at[0, c], dk_r.at[peer[d], c], near(d)).wait_recv()

    def own_dk(j, c):
        return pltpu.make_async_copy(block_head(dsum, (slice(None),), j, c), kv_out.at[:, :, wide_head(r, c)], dk_s.at[j, c])

    def hand(j, own, other):
        @pl.when(r == j)
        def _():
            own()

        @pl.when(r != j)
        def _():
            other()

    def gx_copy(df, n, c):
        return remote(
            gw_out.at[side(df), n, :, head(c)], gw_in.at[fsdp - df, n, :, head(c)], gx_s.at[df, n, c], gx_r.at[fsdp - df, n, c],
            dev(p, r, side(df)),
        )

    def gx_came(df, n, c):
        here = gw_in.at[df, n, :, head(c)]
        remote(here, here, gx_s.at[df, n, c], gx_r.at[df, n, c], dev(p, r, side(df))).wait_recv()

    group = lax.div(p, 2)
    far_first = [lax.rem(2 * (group + 1) + i, planes) for i in range(planes - 2)] + [p + 1 - 2 * lax.rem(p, 2), p]

    def to_partner(n):
        return jnp.logical_or(jnp.logical_and(lower, n > p), jnp.logical_and(upper, n < p))

    def to_plane(n):
        return jnp.logical_or(jnp.logical_and(lower, n < p), jnp.logical_and(upper, n > p))

    def pin_copy(n, c):
        return remote(zw_out.at[n, :, head(c)], pin.at[n, :, head(c)], pin_s.at[n, c], pin_r.at[n, c], partner)

    def tin_copy(n, c):
        return remote(zw_out.at[n, :, head(c)], tin.at[group, :, head(c)], tin_s.at[n, c], tin_r.at[group, c], dev(n, r, f))

    def tin_came(k, c):
        here = tin.at[k, :, head(c)]
        remote(here, here, tin_s.at[0, c], tin_r.at[k, c], partner).wait_recv()

    def f_copy(d, c):
        return remote(fin_out.at[peer[d], :, head(c)], fin_in.at[r, :, head(c)], f_s.at[d, c], f_r.at[d, c], near(d))

    def f_came(d, c):
        here = fin_in.at[peer[d], :, head(c)]
        remote(here, here, f_s.at[d, c], f_r.at[d, c], near(d)).wait_recv()

    around = range(1, SPAN)

    def spread_kv(c):
        for d in around:
            kv_copy(d, c).start()

    def spread_q(c):
        for d in around:
            q_copy(d, c).start()

        @pl.when(not_first)
        def _():
            qz_copy(0, c).start()

    def halo(c):
        @pl.when(not_last)
        def _():
            kz_copy(0, c).start()

    def columns(c):
        def go():
            for df in range(1, fsdp):
                w_copy(df, c).start()

        if by_side(c) is None:
            go()
        else:
            pl.when(by_side(c))(go)

    def pass_columns():
        for c in (heads - 2, heads - 1):
            @pl.when(by_side(c))
            def _(c=c):
                for df in range(1, fsdp):
                    w_came(df, c)
                    wz_copy(df, c).start()

    def lift():
        for h in range(2):
            up_copy(2, h).start()
        for h in range(2):
            up_copy(1, h).start()

    halo(0)
    halo(1)
    spread_kv(0)
    spread_q(0)
    columns(0)
    columns(2)
    spread_q(1)
    columns(3)
    lift()
    spread_q(2)
    spread_kv(1)
    halo(2)
    spread_q(3)
    halo(3)
    spread_kv(2)
    columns(1)
    spread_kv(3)
    row = lax.broadcasted_iota(jnp.int32, (toks, keys), 0)
    col = lax.broadcasted_iota(jnp.int32, (toks, keys), 1)
    for b in range(SPAN):
        first = jnp.where(not_first, 0, plane_toks - b * toks)
        bias[b] = jnp.where((col > row) & (col <= row + plane_toks) & (col >= first), 0.0, NEGATIVE)
    dkv[...] = jnp.zeros(dkv.shape, F32)
    stats[...] = jnp.zeros(stats.shape, F32)

    @pl.when(p == 0)
    def _():
        kv[:, :plane_toks] = jnp.zeros((2, plane_toks, quarter), BF16)

    def forward(c):
        for d in around:
            kv_came(d, c)

            @pl.when(not_last)
            def _(d=d):
                kz_copy(d, c).start()

    def forward_q(c):
        for d in around:
            q_came(d, c)

            @pl.when(not_first)
            def _(d=d):
                qz_copy(d, c).start()

    diagonal = lax.broadcasted_iota(jnp.int32, (toks, toks), 0) == lax.broadcasted_iota(jnp.int32, (toks, toks), 1)

    def as_row(column):
        return jnp.sum(jnp.where(diagonal, column, 0.0), axis=0, keepdims=True)

    def window(b):
        return pl.ds(b * toks, keys)

    def attend(c):
        @pl.when(not_first)
        def _():
            for d in range(SPAN):
                here = kv.at[:, rows(peer[d]), head(c)]
                remote(here, here, kz_s.at[d, c], kz_r.at[d, c], near(1)).wait_recv()

        for b in range(SPAN):
            block = pl.ds(b * toks, toks)
            scores = lax.dot_general(q[block, head(c)], kv[0, window(b), head(c)], NT, preferred_element_type=F32) * inv_root + bias[b]
            top = jnp.max(scores, axis=-1, keepdims=True)
            lifted = jnp.exp(scores - top)
            mass = jnp.sum(lifted, axis=-1, keepdims=True)
            stats[c, 0:1, block] = as_row(top + jnp.log(mass))
            prob = (lifted * (1.0 / mass)).astype(BF16)
            low[c * SPAN + b] = prob
            att[block, head(c)] = jnp.dot(prob, kv[1, window(b), head(c)], preferred_element_type=F32).astype(BF16)

    def center_of(block, c):
        return jnp.sum(ga[block, head(c)].astype(F32) * att[block, head(c)].astype(F32), axis=-1, keepdims=True)

    def send_down(c):
        @pl.when(not_first)
        def _():
            for b in range(SPAN):
                block = pl.ds(b * toks, toks)
                stats[c, 1:2, block] = as_row(center_of(block, c))
            ga_copy(c).start()
            stats_copy(c).start()

    def backward(c):
        for b in range(SPAN):
            block = pl.ds(b * toks, toks)
            g = ga[block, head(c)]
            prob = low[c * SPAN + b]
            k = kv[0, window(b), head(c)]
            products = lax.dot_general(g, kv[1, window(b), head(c)], NT, preferred_element_type=F32)
            ds = (prob.astype(F32) * (products - center_of(block, c))).astype(BF16)
            dq[block, head(c)] = (jnp.dot(ds, k, preferred_element_type=F32) * inv_root).astype(BF16)
            seen = slice(plane_toks - b * toks, keys)
            mine = slice(0, (b + 1) * toks)
            dkv[0, mine, head(c)] += lax.dot_general(ds[:, seen], q[block, head(c)], TN, preferred_element_type=F32) * inv_root
            dkv[1, mine, head(c)] += lax.dot_general(prob[:, seen], g, TN, preferred_element_type=F32)
        for j in range(SPAN):
            hand(j, lambda: own_dq(j, c).start(), lambda: dq_copy(j, c).start())

    def next_plane(c):
        @pl.when(not_last)
        def _():
            for d in range(SPAN):
                here = q_next.at[rows(peer[d]), head(c)]
                remote(here, here, qz_s.at[d, c], qz_r.at[d, c], near(1)).wait_recv()
            ga_copy(c).wait_recv()
            stats_copy(c).wait_recv()
            for b in range(SPAN):
                block = pl.ds(b * toks, toks)
                count = plane_toks - b * toks
                mine = slice(b * toks, plane_toks)
                seen = slice(plane_toks + b * toks, 2 * plane_toks)
                shape = (count, toks)
                visible = lax.broadcasted_iota(jnp.int32, shape, 0) > lax.broadcasted_iota(jnp.int32, shape, 1)
                qn, gn = q_next[block, head(c)], ga_next[block, head(c)]
                scores = lax.dot_general(kv[0, seen, head(c)], qn, NT, preferred_element_type=F32) * inv_root
                prob = jnp.exp(jnp.where(visible, scores - stats_next[c, 0:1, block], NEGATIVE))
                products = lax.dot_general(kv[1, seen, head(c)], gn, NT, preferred_element_type=F32)
                ds = (prob * (products - stats_next[c, 1:2, block])).astype(BF16)
                dkv[0, mine, head(c)] += jnp.dot(ds, qn, preferred_element_type=F32) * inv_root
                dkv[1, mine, head(c)] += jnp.dot(prob.astype(BF16), gn, preferred_element_type=F32)

    def return_kv(c):
        dsum[:, :, head(c)] = dkv[:, :, head(c)].astype(BF16)
        for j in range(SPAN):
            hand(j, lambda: own_dk(j, c).start(), lambda: dk_copy(j, c).start())

    def project(c, d):
        if d == 0:
            for df in range(1, fsdp):
                if by_side(c) is None:
                    w_came(df, c)
                else:
                    pl.when(jnp.logical_not(by_side(c)))(lambda df=df: wz_copy(df, c).wait_recv())
        ga[rows(peer[d]), head(c)] = jnp.dot(up[rows(peer[d]), :], w[:, head(c)], preferred_element_type=F32).astype(BF16)

    def turn(d):
        up_t[:, rows(peer[d])] = up[rows(peer[d]), :].T

    tile = up_in.shape[1] // planes

    def weigh(c):
        for n in far_first:
            rows_n = pl.ds(pl.multiple_of(n * tile, tile), tile)
            value = jnp.dot(up_t[rows_n, :], att[:, head(c)], preferred_element_type=F32)
            value = value.reshape(SPAN, fsdp, own_rows, HEAD_DIM)
            for i in range(fsdp):
                gw_out[i, n, :, head(c)] = value[:, i].reshape(plane_rows, HEAD_DIM).astype(BF16)
            for df in range(1, fsdp):
                gx_copy(df, n, c).start()

    def merge(c):
        for n in far_first:
            total = gw_out[f, n, :, head(c)].astype(F32)
            for df in range(1, fsdp):
                gx_came(df, n, c)
                total = total + gw_in[df, n, :, head(c)].astype(F32)
            zw_out[n, :, head(c)] = total.astype(BF16)

            @pl.when(to_partner(n))
            def _(n=n):
                pin_copy(n, c).start()

    def relay(c):
        for n in range(planes):
            @pl.when(to_plane(n))
            def _(n=n):
                pin_copy(n, c).wait_recv()
                zw_out[n, :, head(c)] = (zw_out[n, :, head(c)].astype(F32) + pin[n, :, head(c)].astype(F32)).astype(BF16)
                tin_copy(n, c).start()

    def total_up(c):
        pin_copy(p, c).wait_recv()
        total = zw_out[p, :, head(c)].astype(F32) + pin[p, :, head(c)].astype(F32)
        for dk in range(1, planes // 2):
            k = lax.rem(group + dk, planes // 2)
            tin_came(k, c)
            total = total + tin[k, :, head(c)].astype(F32)
        for n in range(SPAN):
            fin_out[n, :, head(c)] = total[n * own_rows : (n + 1) * own_rows].astype(BF16)
        for d in (2, 3, 1):
            f_copy(d, c).start()

    def finish(c):
        for d in around:
            f_came(d, c)
        out_w[:, wide_head(r, c)] = fin_out[r, :, head(c)].astype(F32)
        for d in around:
            out_w[:, wide_head(peer[d], c)] = fin_in[peer[d], :, head(c)].astype(F32)

    def drain():
        for c in range(heads):
            for d in around:
                kv_copy(d, c).wait_send()
                q_copy(d, c).wait_send()
            for df in range(1, fsdp):
                if by_side(c) is None:
                    w_copy(df, c).wait_send()
                else:
                    @pl.when(by_side(c))
                    def _(c=c, df=df):
                        w_copy(df, c).wait_send()
                        wz_copy(df, c).wait_send()

            @pl.when(not_last)
            def _(c=c):
                for d in range(SPAN):
                    kz_copy(d, c).wait_send()

            @pl.when(not_first)
            def _(c=c):
                for d in range(SPAN):
                    qz_copy(d, c).wait_send()

        for d in around:
            for h in range(2):
                up_copy(d, h).wait_send()

    def settle():
        kv[:, own_plane(r), :] = kv_in[:, :, quart(r)]
        for copy in own_copies:
            copy.wait()
        for h in range(2):
            up_came(1, h)
        turn(0)
        turn(1)

    def lift_on(h):
        up_came(2, h)
        up_copy(3, h).start()

    def lift_end():
        turn(2)
        for h in range(2):
            up_came(3, h)
        turn(3)

    def project_chip(c):
        project(c, 0)
        project(c, 1)

    def project_rest(c):
        project(c, 2)
        project(c, 3)

    forward(0)
    settle()
    forward_q(1)
    project_chip(0)
    forward_q(0)
    pass_columns()
    attend(0)
    lift_on(0)
    lift_on(1)
    forward_q(2)
    lift_end()
    project_rest(0)
    weigh(0)
    project_chip(2)
    send_down(0)
    project_chip(1)
    forward(1)
    project_chip(3)
    project_rest(2)
    backward(0)
    forward_q(3)
    forward(2)
    project_rest(1)
    merge(0)
    attend(1)
    send_down(1)
    weigh(1)
    backward(1)
    forward(3)
    attend(2)
    send_down(2)
    weigh(2)
    relay(0)
    next_plane(0)
    merge(1)
    backward(2)
    next_plane(2)
    attend(3)
    total_up(0)
    merge(2)
    project_rest(3)
    return_kv(2)
    relay(1)
    weigh(3)
    finish(0)
    return_kv(0)
    send_down(3)
    total_up(1)
    next_plane(1)
    return_kv(1)
    relay(2)
    merge(3)
    backward(3)
    next_plane(3)
    relay(3)
    return_kv(3)
    total_up(2)
    finish(1)
    drain()
    total_up(3)
    finish(2)
    finish(3)
    for c in range(heads):
        for d in around:
            dq_came(d, c)
            dk_came(d, c)
            f_copy(d, c).wait_send()
        for j in range(SPAN):
            hand(j, lambda: own_dq(j, c).wait(), lambda: dq_copy(j, c).wait_send())
            hand(j, lambda: own_dk(j, c).wait(), lambda: dk_copy(j, c).wait_send())
        for df in range(1, fsdp):
            for n in range(planes):
                gx_copy(df, n, c).wait_send()
        for n in range(planes):
            @pl.when(to_partner(n))
            def _(n=n, c=c):
                pin_copy(n, c).wait_send()

            @pl.when(to_plane(n))
            def _(n=n, c=c):
                tin_copy(n, c).wait_send()

        @pl.when(not_first)
        def _(c=c):
            ga_copy(c).wait_send()
            stats_copy(c).wait_send()


def hand_over_kernel(dq_in, kv_in, w_in, dq_out, kv_out, w_out):
    dq_out[...] = dq_in[...]
    w_out[...] = w_in[...]
    for n in range(2):
        kv_out[:, n, :] = kv_in[n]


def hand_over(dq, kv, w):
    toks, width = dq.shape
    steps = 2
    part = toks // steps
    whole = pl.BlockSpec(w.shape, lambda i: (0, 0))
    piece = pl.BlockSpec((part, width), lambda i: (i, 0))
    return pl.pallas_call(
        hand_over_kernel,
        grid=(steps,),
        out_shape=(
            jax.ShapeDtypeStruct(dq.shape, dq.dtype),
            jax.ShapeDtypeStruct((toks, 2, width), kv.dtype),
            jax.ShapeDtypeStruct(w.shape, w.dtype),
        ),
        in_specs=[piece, pl.BlockSpec((2, part, width), lambda i: (0, i, 0)), whole],
        out_specs=(piece, pl.BlockSpec((part, 2, width), lambda i: (i, 0, 0)), whole),
        name="hand_over",
    )(dq, kv, w)


def shards(queries, keys_values, upstream, out_weight):
    seqs, toks, width = queries.shape
    ctx, fsdp = lax.axis_size("ctx"), lax.axis_size("fsdp")
    planes = ctx // SPAN
    model = upstream.shape[2]
    own_rows = model // (ctx * fsdp)
    quarter = width // SPAN
    heads = quarter // HEAD_DIM
    group = SPAN * toks
    dma = pltpu.SemaphoreType.DMA
    any_spec = pl.BlockSpec(memory_space=pl.ANY)
    vm = pl.BlockSpec(memory_space=pltpu.VMEM)
    near = dma((SPAN, heads))
    sides = dma((fsdp, heads))
    levels = dma((planes, heads))
    parts = dma((fsdp, planes, heads))
    dq, out_kv, out_w = pl.pallas_call(
        functools.partial(layer_kernel, planes, fsdp),
        out_shape=(
            jax.ShapeDtypeStruct((toks, width), BF16),
            jax.ShapeDtypeStruct((2, toks, width), BF16),
            jax.ShapeDtypeStruct((own_rows, width), F32),
        ),
        in_specs=[any_spec] * 4,
        out_specs=(any_spec, any_spec, vm),
        scratch_shapes=[
            pltpu.VMEM((toks, 2, width), BF16),
            pltpu.VMEM((2, toks, width), BF16),
            pltpu.VMEM((group, quarter), BF16),
            pltpu.VMEM((2, 2 * group, quarter), BF16),
            pltpu.VMEM((group, model), BF16),
            pltpu.VMEM((model, group), BF16),
            pltpu.VMEM((model, quarter), BF16),
            pltpu.VMEM((group, quarter), BF16),
            pltpu.VMEM((group, quarter), BF16),
            pltpu.VMEM((heads * SPAN, toks, group + toks), BF16),
            pltpu.VMEM((SPAN, toks, group + toks), F32),
            pltpu.VMEM((group, quarter), BF16),
            pltpu.VMEM((2, group, quarter), F32),
            pltpu.VMEM((2, group, quarter), BF16),
            pltpu.VMEM((group, quarter), BF16),
            pltpu.VMEM((group, quarter), BF16),
            pltpu.VMEM((heads, 8, group), F32),
            pltpu.VMEM((heads, 8, group), F32),
            pltpu.VMEM((fsdp, planes, SPAN * own_rows, quarter), BF16),
            pltpu.VMEM((fsdp, planes, SPAN * own_rows, quarter), BF16),
            pltpu.VMEM((planes, SPAN * own_rows, quarter), BF16),
            pltpu.VMEM((planes, SPAN * own_rows, quarter), BF16),
            pltpu.VMEM((planes // 2, SPAN * own_rows, quarter), BF16),
            pltpu.VMEM((SPAN, own_rows, quarter), BF16),
            pltpu.VMEM((SPAN, own_rows, quarter), BF16),
            dma((4,)), near, near, near, near, dma((SPAN, 2)), dma((SPAN, 2)), sides, sides, sides, sides, near, near,
            near, near, near, near, near, near, dma((heads,)), dma((heads,)), dma((heads,)), dma((heads,)), parts, parts, levels, levels, levels, dma((planes // 2, heads)), near, near,
        ],
        compiler_params=pltpu.CompilerParams(collective_id=0, has_side_effects=True),
        name="layer",
    )(queries[0], keys_values[0], upstream[0], out_weight)
    dq, out_kv, out_w = hand_over(dq, out_kv, out_w)
    return dq[None], out_kv[None], out_w


def solution(mesh):
    return jax.shard_map(
        shards,
        mesh=mesh,
        in_specs=(
            P("fsdp", "ctx", None),
            P("fsdp", "ctx", None, None),
            P("fsdp", "ctx", None),
            P("fsdp", None),
        ),
        out_specs=(P("fsdp", "ctx", None), P("fsdp", "ctx", None, None), P(("ctx", "fsdp"), None)),
        check_vma=False,
    )
```
